256 devices in a mesh: col: 64 (over y, z, core), row: 4 (over x).
Axes of the slice: x: 4, y: 4, z: 8, core: 2. Of those that a mesh axis runs over, the one named last changes fastest.
Arguments:
- r_slab: float32 [1024, 16384], P('row', 'col'), may hold values from -4 to 8, as said below
- arc_rows: float32 [4096, 16384], P('row', 'col'), may hold values from -6 to 6
- arc_blocks: int32 [32, 64], P('row', 'col'), may hold values 0 or 1
Outputs:
- r_updated: float32 [1024, 16384], P('row', 'col')
The draws below stay inside these ranges and needn't reach their ends.
Inputs may be any that keep to these rules, and one draw needn't show every extreme that they name: r_slab is zero wherever an entry's global column index is below its row index, and its diagonal is positive.
All inputs are finite; a program needn't handle non-finite values. No bound on the sum of `arc_blocks` on one device may be relied on, other than what follows from the above.
Results may differ from the reference program's by a relative error of at most 0.000098.
Values sent between devices are 32-bit elements; how exact they have to be, the bound alone decides.
A program may use at most 64 MiB of HBM per device.

```python
import jax
import jax.numpy as jnp
from jax import lax

B = 256
P_SIZE = 4
ARC_ROWS = 128
BLK_DEV = 1
NBLK = 64
NC = 16384
ROWS = 4096
ARCS = 32
N_COL = 64


def draw_r_slab(key, part):
    first_key, second_key = jax.random.split(jax.random.fold_in(key, 11))
    shape = (P_SIZE * B, NBLK * B)
    row_ids = lax.broadcasted_iota(jnp.int32, shape, 0)
    col_ids = lax.broadcasted_iota(jnp.int32, shape, 1)
    stored = col_ids // B
    inner = col_ids % B
    owner = stored // BLK_DEV
    local = stored % BLK_DEV
    global_col = (local * N_COL + owner) * B + inner
    above = jnp.clip(jax.random.normal(first_key, shape, jnp.float32), -4.0, 4.0)
    diagonal = jax.random.uniform(second_key, shape, jnp.float32, 2.0, 6.0)
    zeros = jnp.zeros(shape, jnp.float32)
    return jnp.where(global_col > row_ids, above, jnp.where(global_col == row_ids, diagonal, zeros)).astype(jnp.float32)


def touch_ends(drawn, own_key, least, largest):
    place = [jax.random.randint(jax.random.fold_in(own_key, axis), (), 0, length) for axis, length in enumerate(drawn.shape)]
    widest = drawn.shape.index(max(drawn.shape))
    next_to = place[:widest] + [(place[widest] + 1) % drawn.shape[widest]] + place[widest + 1:]
    return drawn.at[tuple(place)].set(least).at[tuple(next_to)].set(largest)


def steps_of(own_key, extent, cuts, smallest, largest):
    gain, own = 1.0, jax.random.fold_in(own_key, 6)
    for axis_at, blocks in cuts:
        heights = jnp.exp(jax.random.uniform(jax.random.fold_in(own, axis_at), (blocks,), jnp.float32, smallest / len(cuts), largest / len(cuts)))
        gain = gain * jnp.repeat(heights, extent[axis_at] // blocks).reshape([-1 if axis == axis_at else 1 for axis in range(len(extent))])
    return gain


def gaussian(stream_key, extent, width, most, shards=(), held_as=jnp.bfloat16):
    values = jax.random.normal(stream_key, extent, jnp.float32) * width
    if len(shards) > 0:
        values = steps_of(stream_key, extent, shards, -0.22, 0.18) * values
    return jnp.clip(values, min=-most, max=most).astype(held_as)


def setup_inputs(seed: int = 0) -> dict:
    streams_of = jax.random.split(jax.random.key(seed), 4)
    r_slab = draw_r_slab(jax.random.fold_in(streams_of[3], 71), 0)
    arc_rows = gaussian(streams_of[1], (ROWS, NC), 1.0, 6.0, ((0, 4), (1, 64)), jnp.float32)
    arc_blocks = touch_ends((jax.random.randint(streams_of[2], (ARCS, NBLK), 0, 2) < 1).astype(jnp.int32), jax.random.fold_in(streams_of[2], 1), 0, 1)
    return dict(r_slab=r_slab, arc_rows=arc_rows, arc_blocks=arc_blocks)


def to_global(field):
    height = field.shape[0]
    return field.reshape(height, N_COL, BLK_DEV, B).transpose(0, 2, 1, 3).reshape(height, NBLK * B)

def to_storage(field):
    height = field.shape[0]
    return field.reshape(height, BLK_DEV, N_COL, B).transpose(0, 2, 1, 3).reshape(height, NBLK * B)

def reference(r_slab, arc_rows, arc_blocks):
    live = arc_blocks.astype(jnp.float32)
    masked = (arc_rows.reshape(ARCS, ARC_ROWS, NBLK, B) * live[:, None, :, None]).reshape(ROWS, NBLK * B)
    slab = to_global(r_slab)
    rows = to_global(masked)
    lead = P_SIZE * B
    gram = jnp.dot(slab[:, :lead].T, slab, precision=lax.Precision.HIGHEST)
    gram = gram + jnp.dot(rows[:, :lead].T, rows, precision=lax.Precision.HIGHEST)
    lower = jnp.linalg.cholesky(gram[:, :lead])
    factor = jax.scipy.linalg.solve_triangular(lower, gram, lower=True)
    row_ids = lax.broadcasted_iota(jnp.int32, factor.shape, 0)
    col_ids = lax.broadcasted_iota(jnp.int32, factor.shape, 1)
    factor = jnp.where(col_ids >= row_ids, factor, jnp.zeros_like(factor))
    return to_storage(factor)
```

```python
import jax
import jax.numpy as jnp
from jax import lax
from jax.sharding import PartitionSpec as P

B = 256
P_SIZE = 4
ARC_ROWS = 128
HI = lax.Precision.HIGHEST


def inner_dot(left, right):
    return lax.dot_general(left, right, (((0,), (0,)), ((), ())), precision=HI)


def plain_dot(left, right):
    return jnp.dot(left, right, precision=HI)


def on_device(r_slab, arc_rows, arc_blocks):
    n_col = lax.axis_size("col")
    col_index = lax.axis_index("col")
    row_index = lax.axis_index("row")
    n_arcs, blocks_here = arc_blocks.shape
    lead = P_SIZE * B
    live = arc_blocks.astype(jnp.float32)
    masked = (arc_rows.reshape(n_arcs, ARC_ROWS, blocks_here, B) * live[:, None, :, None]).reshape(
        arc_rows.shape
    )
    stacked = jnp.concatenate([r_slab, masked], axis=0)
    height = stacked.shape[0]
    part = height // n_col
    pieces = stacked.reshape(n_col, part, B)
    pieces = lax.all_to_all(pieces, "col", split_axis=0, concat_axis=0, tiled=True)
    mine = pieces[:P_SIZE]
    panels = lax.all_gather(mine, "col")
    panels = panels.transpose(0, 2, 1, 3).reshape(height, lead)
    share = lead // n_col
    own = lax.dynamic_slice(panels, (0, col_index * share), (height, share))
    gram_part = lax.psum(inner_dot(own, panels), "row")
    gram = lax.all_gather(gram_part, "col", tiled=True)
    rhs = lax.psum(inner_dot(panels, stacked), "row")
    lower = jnp.linalg.cholesky(gram, symmetrize_input=False)
    factor = jax.scipy.linalg.solve_triangular(lower, rhs, lower=True)
    mine_out = lax.dynamic_slice(factor, (row_index * B, 0), (B, B))
    row_ids = row_index * B + lax.broadcasted_iota(jnp.int32, (B, B), 0)
    col_ids = col_index * B + lax.broadcasted_iota(jnp.int32, (B, B), 1)
    return jnp.where(col_ids >= row_ids, mine_out, jnp.zeros_like(mine_out))


def solution(mesh):
    return jax.shard_map(
        on_device,
        mesh=mesh,
        in_specs=(P("row", "col"), P("row", "col"), P("row", "col")),
        out_specs=P("row", "col"),
        check_vma=False,
    )
```

```python
import jax
import jax.numpy as jnp
from jax import lax
from jax.experimental import pallas as pl
from jax.experimental.pallas import tpu as pltpu
from jax.sharding import PartitionSpec as P

B = 256
P_SIZE = 4
ARC_ROWS = 128
HI = lax.Precision.HIGHEST
TILE = 128
GROUP = 16


def inner_dot(left, right):
    return lax.dot_general(left, right, (((0,), (0,)), ((), ())), precision=HI)


def plain_dot(left, right):
    return jnp.dot(left, right, precision=HI)


def eliminate_tile(work_ref, inv_ref):
    row_of = lax.broadcasted_iota(jnp.int32, (GROUP, 2 * TILE), 0)
    lane_of = lax.broadcasted_iota(jnp.int32, (GROUP, TILE), 1)
    narrow_row = row_of[:, :TILE]
    for start in range(0, TILE, GROUP):
        panel = work_ref[start:start + GROUP, :]
        spread = [
            jnp.broadcast_to(panel[:, start + i:start + i + 1], (GROUP, TILE)) for i in range(GROUP)
        ]
        left, right = panel[:, :TILE], panel[:, TILE:]
        pivots = jnp.ones((GROUP, TILE), jnp.float32)
        for i in range(GROUP):
            pivot = spread[i][i:i + 1, :]
            pivots = jnp.where(narrow_row == i, jnp.broadcast_to(pivot, pivots.shape), pivots)
            if i + 1 == GROUP:
                break
            scale = jnp.where(narrow_row > i, spread[i], 0.0) * (1.0 / pivot)
            for later in range(i + 1, GROUP):
                spread[later] = spread[later] - scale * spread[later][i:i + 1, :]
            left = left - scale * left[i:i + 1, :]
            right = right - scale * right[i:i + 1, :]
        root = 1.0 / jnp.sqrt(pivots)
        left, right = left * root, right * root
        inv_ref[start:start + GROUP, :] = right
        if start + GROUP < TILE:
            rest = jnp.where(lane_of >= start + GROUP, left, 0.0)
            both = jnp.concatenate([left, right], axis=1)
            work_ref[...] = work_ref[...] - lax.dot_general(
                rest, both, (((0,), (0,)), ((), ())), precision=HI, preferred_element_type=jnp.float32
            )

def inverse_kernel(gram_ref, out_ref, work_ref, inv_ref):
    size = gram_ref.shape[0]
    tiles = size // TILE
    out_ref[...] = gram_ref[...]
    eye = jnp.where(
        lax.broadcasted_iota(jnp.int32, (TILE, TILE), 0)
        == lax.broadcasted_iota(jnp.int32, (TILE, TILE), 1), 1.0, 0.0
    ).astype(jnp.float32)

    def step(k, carry):
        at = pl.multiple_of(k * TILE, TILE)
        work_ref[:, :TILE] = out_ref[pl.ds(at, TILE), pl.ds(at, TILE)]
        work_ref[:, TILE:] = eye
        eliminate_tile(work_ref, inv_ref)
        out_ref[pl.ds(at, TILE), pl.ds(at, TILE)] = eye
        out_ref[pl.ds(at, TILE), :] = jnp.dot(
            inv_ref[...], out_ref[pl.ds(at, TILE), :], precision=HI, preferred_element_type=jnp.float32
        )

        def update(i, inner):
            below = pl.multiple_of(i * TILE, TILE)
            out_ref[pl.ds(below, TILE), pl.ds(at, TILE)] = jnp.zeros((TILE, TILE), jnp.float32)
            out_ref[pl.ds(below, TILE), :] = out_ref[pl.ds(below, TILE), :] - lax.dot_general(
                out_ref[pl.ds(at, TILE), pl.ds(below, TILE)],
                out_ref[pl.ds(at, TILE), :],
                (((0,), (0,)), ((), ())),
                precision=HI,
                preferred_element_type=jnp.float32,
            )
            return inner

        lax.fori_loop(k + 1, tiles, update, 0)
        return carry

    lax.fori_loop(0, tiles, step, 0)

def block_inverse(gram):
    size = gram.shape[0]
    return pl.pallas_call(
        inverse_kernel,
        out_shape=jax.ShapeDtypeStruct(gram.shape, jnp.float32),
        in_specs=[pl.BlockSpec(memory_space=pltpu.VMEM)],
        out_specs=pl.BlockSpec(memory_space=pltpu.VMEM),
        scratch_shapes=[pltpu.VMEM((TILE, 2 * TILE), jnp.float32), pltpu.VMEM((TILE, TILE), jnp.float32)],
        cost_estimate=pl.CostEstimate(flops=8 * size**3, bytes_accessed=8 * size**2, transcendentals=0),
        name="block_inverse",
    )(gram)


def on_device(r_slab, arc_rows, arc_blocks):
    n_col = lax.axis_size("col")
    col_index = lax.axis_index("col")
    row_index = lax.axis_index("row")
    n_arcs, blocks_here = arc_blocks.shape
    lead = P_SIZE * B
    live = arc_blocks.astype(jnp.float32)
    masked = (arc_rows.reshape(n_arcs, ARC_ROWS, blocks_here, B) * live[:, None, :, None]).reshape(
        arc_rows.shape
    )
    stacked = jnp.concatenate([r_slab, masked], axis=0)
    height = stacked.shape[0]
    part = height // n_col
    pieces = stacked.reshape(n_col, part, B)
    pieces = lax.all_to_all(pieces, "col", split_axis=0, concat_axis=0, tiled=True)
    mine = pieces[:P_SIZE]
    panels = lax.all_gather(mine, "col")
    panels = panels.transpose(0, 2, 1, 3).reshape(height, lead)
    share = lead // n_col
    own = lax.dynamic_slice(panels, (0, col_index * share), (height, share))
    gram_part = lax.psum(inner_dot(own, panels), "row")
    gram = lax.all_gather(gram_part, "col", tiled=True)
    rhs, gram = lax.optimization_barrier((inner_dot(panels, stacked), gram))
    rhs = lax.psum(rhs, "row")
    inverse = block_inverse(gram)
    inverse = lax.dynamic_slice(inverse, (row_index * B, 0), (B, lead))
    tile_row = (row_index * B + lax.broadcasted_iota(jnp.int32, (B, lead), 0)) // TILE
    tile_col = lax.broadcasted_iota(jnp.int32, (B, lead), 1) // TILE
    inverse = jnp.where(tile_col <= tile_row, inverse, jnp.zeros_like(inverse))
    mine_out = plain_dot(inverse, rhs)
    row_ids = row_index * B + lax.broadcasted_iota(jnp.int32, (B, B), 0)
    col_ids = col_index * B + lax.broadcasted_iota(jnp.int32, (B, B), 1)
    return jnp.where(col_ids >= row_ids, mine_out, jnp.zeros_like(mine_out))


def solution(mesh):
    return jax.shard_map(
        on_device,
        mesh=mesh,
        in_specs=(P("row", "col"), P("row", "col"), P("row", "col")),
        out_specs=P("row", "col"),
        check_vma=False,
    )
```

```python
import jax
import jax.numpy as jnp
from jax import lax
from jax.experimental import pallas as pl
from jax.experimental.pallas import tpu as pltpu
from jax.sharding import PartitionSpec as P

B = 256
P_SIZE = 4
ARC_ROWS = 128
HI = lax.Precision.HIGHEST
TILE = 128
GROUP = 16
X_CHIPS, Y_CHIPS, Z_CHIPS = 4, 4, 8
HALVES = 2
MESH = pl.DeviceIdType.MESH


def inner_dot(left, right):
    return lax.dot_general(left, right, (((0,), (0,)), ((), ())), precision=HI)


def plain_dot(left, right):
    return jnp.dot(left, right, precision=HI)


def eliminate_tile(work_ref, inv_ref):
    row_of = lax.broadcasted_iota(jnp.int32, (GROUP, 2 * TILE), 0)
    lane_of = lax.broadcasted_iota(jnp.int32, (GROUP, TILE), 1)
    narrow_row = row_of[:, :TILE]
    for start in range(0, TILE, GROUP):
        panel = work_ref[start:start + GROUP, :]
        spread = [
            jnp.broadcast_to(panel[:, start + i:start + i + 1], (GROUP, TILE)) for i in range(GROUP)
        ]
        left, right = panel[:, :TILE], panel[:, TILE:]
        pivots = jnp.ones((GROUP, TILE), jnp.float32)
        for i in range(GROUP):
            pivot = spread[i][i:i + 1, :]
            pivots = jnp.where(narrow_row == i, jnp.broadcast_to(pivot, pivots.shape), pivots)
            if i + 1 == GROUP:
                break
            scale = jnp.where(narrow_row > i, spread[i], 0.0) * (1.0 / pivot)
            for later in range(i + 1, GROUP):
                spread[later] = spread[later] - scale * spread[later][i:i + 1, :]
            left = left - scale * left[i:i + 1, :]
            right = right - scale * right[i:i + 1, :]
        root = 1.0 / jnp.sqrt(pivots)
        left, right = left * root, right * root
        inv_ref[start:start + GROUP, :] = right
        if start + GROUP < TILE:
            rest = jnp.where(lane_of >= start + GROUP, left, 0.0)
            both = jnp.concatenate([left, right], axis=1)
            work_ref[...] = work_ref[...] - lax.dot_general(
                rest, both, (((0,), (0,)), ((), ())), precision=HI, preferred_element_type=jnp.float32
            )

def inverse_kernel(gram_ref, out_ref, work_ref, inv_ref):
    size = gram_ref.shape[0]
    tiles = size // TILE
    out_ref[...] = gram_ref[...]
    eye = jnp.where(
        lax.broadcasted_iota(jnp.int32, (TILE, TILE), 0)
        == lax.broadcasted_iota(jnp.int32, (TILE, TILE), 1), 1.0, 0.0
    ).astype(jnp.float32)

    def step(k, carry):
        at = pl.multiple_of(k * TILE, TILE)
        work_ref[:, :TILE] = out_ref[pl.ds(at, TILE), pl.ds(at, TILE)]
        work_ref[:, TILE:] = eye
        eliminate_tile(work_ref, inv_ref)
        out_ref[pl.ds(at, TILE), pl.ds(at, TILE)] = eye
        out_ref[pl.ds(at, TILE), :] = jnp.dot(
            inv_ref[...], out_ref[pl.ds(at, TILE), :], precision=HI, preferred_element_type=jnp.float32
        )

        def update(i, inner):
            below = pl.multiple_of(i * TILE, TILE)
            out_ref[pl.ds(below, TILE), pl.ds(at, TILE)] = jnp.zeros((TILE, TILE), jnp.float32)
            out_ref[pl.ds(below, TILE), :] = out_ref[pl.ds(below, TILE), :] - lax.dot_general(
                out_ref[pl.ds(at, TILE), pl.ds(below, TILE)],
                out_ref[pl.ds(at, TILE), :],
                (((0,), (0,)), ((), ())),
                precision=HI,
                preferred_element_type=jnp.float32,
            )
            return inner

        lax.fori_loop(k + 1, tiles, update, 0)
        return carry

    lax.fori_loop(0, tiles, step, 0)

def block_inverse(gram):
    size = gram.shape[0]
    return pl.pallas_call(
        inverse_kernel,
        out_shape=jax.ShapeDtypeStruct(gram.shape, jnp.float32),
        in_specs=[pl.BlockSpec(memory_space=pltpu.VMEM)],
        out_specs=pl.BlockSpec(memory_space=pltpu.VMEM),
        scratch_shapes=[pltpu.VMEM((TILE, 2 * TILE), jnp.float32), pltpu.VMEM((TILE, TILE), jnp.float32)],
        cost_estimate=pl.CostEstimate(flops=8 * size**3, bytes_accessed=8 * size**2, transcendentals=0),
        name="block_inverse",
    )(gram)


def ring_places():
    me = lax.axis_index("col")
    return me % 2, me // 2 // Z_CHIPS, (me // 2) % Z_CHIPS


def col_of(core, y, z):
    return (y * Z_CHIPS + z) * 2 + core


def relay_rings(piece, send_sems, recv_sems):
    core, y, z = ring_places()
    sent = []

    def pass_on(slot, src_y, src_z, to):
        copy = pltpu.make_async_remote_copy(
            src_ref=piece(core, src_y, src_z),
            dst_ref=piece(core, src_y, src_z),
            send_sem=send_sems.at[slot],
            recv_sem=recv_sems.at[slot],
            device_id={"col": to},
            device_id_type=MESH,
        )
        copy.start()
        sent.append(copy)

    def arrived(slot, src_core, src_y, src_z):
        here = piece(src_core, src_y, src_z)
        pltpu.make_async_copy(here, here, recv_sems.at[slot]).wait()

    z_up, z_down = (z + 1) % Z_CHIPS, (z + Z_CHIPS - 1) % Z_CHIPS
    y_up, y_down = (y + 1) % Y_CHIPS, (y + Y_CHIPS - 1) % Y_CHIPS
    y_far = (y + 2) % Y_CHIPS
    twin = col_of(1 - core, y, z)
    slots_z, slots_up, slots_down, slots_far, slots_twin = 0, 8, 16, 24, 32
    order = [0, 1, 7, 2, 6, 3, 5, 4]

    def source(back):
        return (z + Z_CHIPS - back) % Z_CHIPS

    def spread_y(back):
        pass_on(slots_up + back, y, source(back), col_of(core, y_up, z))
        pass_on(slots_down + back, y, source(back), col_of(core, y_down, z))
        pass_on(slots_twin + back, y, source(back), twin)

    def spread_far(back):
        arrived(slots_up + back, core, y_down, source(back))
        if back % 2 == 0:
            pass_on(slots_far + back, y_down, source(back), col_of(core, y_up, z))
        pass_on(slots_twin + 8 + back, y_down, source(back), twin)
        arrived(slots_down + back, core, y_up, source(back))
        if back % 2 == 1:
            pass_on(slots_far + back, y_up, source(back), col_of(core, y_down, z))
        pass_on(slots_twin + 16 + back, y_up, source(back), twin)

    def spread_twin(back):
        arrived(slots_far + back, core, y_far, source(back))
        pass_on(slots_twin + 24 + back, y_far, source(back), twin)

    pass_on(slots_z + 1, y, z, col_of(core, y, z_up))
    pass_on(slots_z + 7, y, z, col_of(core, y, z_down))
    spread_y(0)
    for at, back in enumerate(order):
        if back:
            arrived(slots_z + back, core, y, source(back))
            if back < 4:
                pass_on(slots_z + back + 1, y, source(back), col_of(core, y, z_up))
            if back > 5:
                pass_on(slots_z + back - 1, y, source(back), col_of(core, y, z_down))
            spread_y(back)
        if at >= 2:
            spread_far(order[at - 2])
        if at >= 4:
            spread_twin(order[at - 4])
    for back in order[6:]:
        spread_far(back)
    for back in order[4:]:
        spread_twin(back)
    for back in order:
        for kind, src_y in enumerate((y, y_down, y_up, y_far)):
            arrived(slots_twin + 8 * kind + back, 1 - core, src_y, source(back))
    for copy in sent:
        copy.wait_send()


def lead_kernel(block_ref, out_ref, own_sem, scatter_send, scatter_recv, send_sems, recv_sems):
    core, y, z = ring_places()
    chip = y * Z_CHIPS + z
    chips = Y_CHIPS * Z_CHIPS
    height = block_ref.shape[0] // chips
    barrier = pltpu.get_barrier_semaphore()

    def greet(step, carry):
        other = (chip + step) % chips
        pl.semaphore_signal(barrier, inc=1, device_id={"col": other * 2 + core}, device_id_type=MESH)
        return carry

    lax.fori_loop(1, chips, greet, 0)
    pl.semaphore_signal(barrier, inc=1, device_id={"col": chip * 2 + 1 - core}, device_id_type=MESH)
    pl.semaphore_wait(barrier, chips)

    def rows(of_chip):
        return pl.ds(pl.multiple_of(of_chip * height, 8), height)

    def scatter_copy(half, to_chip, step):
        return pltpu.make_async_remote_copy(
            src_ref=block_ref.at[rows(to_chip), :],
            dst_ref=out_ref.at[core, half, rows(to_chip), :],
            send_sem=scatter_send.at[step],
            recv_sem=scatter_recv.at[half],
            device_id={"col": to_chip * 2 + core},
            device_id_type=MESH,
        )

    for half in range(HALVES):

        @pl.when(chip == half)
        def _():
            def push(step, carry):
                scatter_copy(half, (half + step) % chips, step).start()
                return carry

            lax.fori_loop(1, chips, push, 0)
            own = pltpu.make_async_copy(
                block_ref.at[rows(half), :], out_ref.at[core, half, rows(half), :], own_sem
            )
            own.start()
            own.wait()

    for half in range(HALVES):

        @pl.when(chip != half)
        def _():
            here = out_ref.at[core, half, rows(chip), :]
            pltpu.make_async_copy(here, here, scatter_recv.at[half]).wait()

    relay_rings(
        lambda of_core, of_y, of_z: out_ref.at[of_core, :, rows(of_y * Z_CHIPS + of_z), :],
        send_sems,
        recv_sems,
    )
    for half in range(HALVES):

        @pl.when(chip == half)
        def _():
            def drain(step, carry):
                scatter_copy(half, (half + step) % chips, step).wait_send()
                return carry

            lax.fori_loop(1, chips, drain, 0)


def gram_kernel(part_ref, out_ref, slots_ref, own_sem, row_send, row_recv, send_sems, recv_sems):
    core, y, z = ring_places()
    row = lax.axis_index("row")
    height = part_ref.shape[0]
    barrier = pltpu.get_barrier_semaphore()
    for near in (
        col_of(core, y, (z + 1) % Z_CHIPS),
        col_of(core, y, (z + Z_CHIPS - 1) % Z_CHIPS),
        col_of(core, (y + 1) % Y_CHIPS, z),
        col_of(core, (y + Y_CHIPS - 1) % Y_CHIPS, z),
        col_of(1 - core, y, z),
    ):
        pl.semaphore_signal(barrier, inc=1, device_id={"col": near}, device_id_type=MESH)
    for step in range(1, X_CHIPS):
        pl.semaphore_signal(barrier, inc=1, device_id={"row": (row + step) % X_CHIPS}, device_id_type=MESH)
    pl.semaphore_wait(barrier, 5 + X_CHIPS - 1)
    copies = []
    for step in range(1, X_CHIPS):
        copy = pltpu.make_async_remote_copy(
            src_ref=part_ref,
            dst_ref=slots_ref.at[row],
            send_sem=row_send.at[step],
            recv_sem=row_recv.at[step],
            device_id={"row": (row + step) % X_CHIPS},
            device_id_type=MESH,
        )
        copy.start()
        copies.append(copy)
    own = pltpu.make_async_copy(part_ref, slots_ref.at[row], own_sem)
    own.start()
    own.wait()
    for step in range(1, X_CHIPS):
        here = slots_ref.at[(row + X_CHIPS - step) % X_CHIPS]
        pltpu.make_async_copy(here, here, row_recv.at[step]).wait()
    total = slots_ref[0]
    for other in range(1, X_CHIPS):
        total = total + slots_ref[other]

    def piece(of_core, of_y, of_z):
        first = pl.multiple_of((of_y * Z_CHIPS + of_z) * height, 8)
        return out_ref.at[of_core, pl.ds(first, height), :]

    piece(core, y, z)[...] = total
    relay_rings(piece, send_sems, recv_sems)
    for copy in copies:
        copy.wait_send()


def spread_lead(block):
    height, width = block.shape
    chips = Y_CHIPS * Z_CHIPS
    return pl.pallas_call(
        lead_kernel,
        out_shape=jax.ShapeDtypeStruct((2, HALVES, height, width), jnp.float32),
        in_specs=[pl.BlockSpec(memory_space=pltpu.VMEM)],
        out_specs=pl.BlockSpec(memory_space=pltpu.VMEM),
        scratch_shapes=[
            pltpu.SemaphoreType.DMA,
            pltpu.SemaphoreType.DMA((chips,)),
            pltpu.SemaphoreType.DMA((HALVES,)),
            pltpu.SemaphoreType.DMA((64,)),
            pltpu.SemaphoreType.DMA((64,)),
        ],
        compiler_params=pltpu.CompilerParams(collective_id=0, has_side_effects=True),
        name="spread_lead",
    )(block)


def sum_gram(part):
    height, width = part.shape
    chips = Y_CHIPS * Z_CHIPS
    return pl.pallas_call(
        gram_kernel,
        out_shape=jax.ShapeDtypeStruct((2, chips * height, width), jnp.float32),
        in_specs=[pl.BlockSpec(memory_space=pltpu.VMEM)],
        out_specs=pl.BlockSpec(memory_space=pltpu.VMEM),
        scratch_shapes=[
            pltpu.VMEM((X_CHIPS, height, width), jnp.float32),
            pltpu.SemaphoreType.DMA,
            pltpu.SemaphoreType.DMA((X_CHIPS,)),
            pltpu.SemaphoreType.DMA((X_CHIPS,)),
            pltpu.SemaphoreType.DMA((64,)),
            pltpu.SemaphoreType.DMA((64,)),
        ],
        compiler_params=pltpu.CompilerParams(collective_id=1, has_side_effects=True),
        name="sum_gram",
    )(part)


def on_device(r_slab, arc_rows, arc_blocks):
    n_col = 2 * Y_CHIPS * Z_CHIPS
    col_index = lax.axis_index("col")
    row_index = lax.axis_index("row")
    n_arcs, blocks_here = arc_blocks.shape
    lead = P_SIZE * B
    live = arc_blocks.astype(jnp.float32)
    masked = (arc_rows.reshape(n_arcs, ARC_ROWS, blocks_here, B) * live[:, None, :, None]).reshape(
        arc_rows.shape
    )
    stacked = jnp.concatenate([r_slab, masked], axis=0)
    panels = spread_lead(stacked)
    share = lead // n_col
    row_start = (col_index % 2) * (lead // 2) + (col_index // 2) * share
    block = row_start // B
    own = lax.dynamic_slice(
        panels, (block % 2, block // 2, 0, row_start % B), (1, 1, stacked.shape[0], share)
    )[0, 0]
    gram_part = jnp.concatenate(
        [inner_dot(own, panels[j % 2, j // 2]) for j in range(P_SIZE)], axis=1
    )
    gram = sum_gram(gram_part).reshape(lead, lead)
    rhs_part = jnp.concatenate(
        [inner_dot(panels[j % 2, j // 2], stacked) for j in range(P_SIZE)], axis=0
    )
    rhs, gram = lax.optimization_barrier((rhs_part, gram))
    rhs = lax.psum(rhs, "row")
    inverse = block_inverse(gram)
    inverse = lax.dynamic_slice(inverse, (row_index * B, 0), (B, lead))
    tile_row = (row_index * B + lax.broadcasted_iota(jnp.int32, (B, lead), 0)) // TILE
    tile_col = lax.broadcasted_iota(jnp.int32, (B, lead), 1) // TILE
    inverse = jnp.where(tile_col <= tile_row, inverse, jnp.zeros_like(inverse))
    mine_out = plain_dot(inverse, rhs)
    row_ids = row_index * B + lax.broadcasted_iota(jnp.int32, (B, B), 0)
    col_ids = col_index * B + lax.broadcasted_iota(jnp.int32, (B, B), 1)
    return jnp.where(col_ids >= row_ids, mine_out, jnp.zeros_like(mine_out))


def solution(mesh):
    return jax.shard_map(
        on_device,
        mesh=mesh,
        in_specs=(P("row", "col"), P("row", "col"), P("row", "col")),
        out_specs=P("row", "col"),
        check_vma=False,
    )
```

```python
import jax
import jax.numpy as jnp
from jax import lax
from jax.experimental import pallas as pl
from jax.experimental.pallas import tpu as pltpu
from jax.sharding import PartitionSpec as P

B = 256
P_SIZE = 4
ARC_ROWS = 128
HI = lax.Precision.HIGHEST
TILE = 128
GROUP = 16
X_CHIPS, Y_CHIPS, Z_CHIPS = 4, 4, 8
HALVES = 2
MESH = pl.DeviceIdType.MESH


def inner_dot(left, right):
    return lax.dot_general(left, right, (((0,), (0,)), ((), ())), precision=HI)


def plain_dot(left, right):
    return jnp.dot(left, right, precision=HI)


def eliminate_tile(work_ref, inv_ref):
    row_of = lax.broadcasted_iota(jnp.int32, (GROUP, 2 * TILE), 0)
    lane_of = lax.broadcasted_iota(jnp.int32, (GROUP, TILE), 1)
    narrow_row = row_of[:, :TILE]
    for start in range(0, TILE, GROUP):
        panel = work_ref[start:start + GROUP, :]
        spread = [
            jnp.broadcast_to(panel[:, start + i:start + i + 1], (GROUP, TILE)) for i in range(GROUP)
        ]
        left, right = panel[:, :TILE], panel[:, TILE:]
        pivots = jnp.ones((GROUP, TILE), jnp.float32)
        for i in range(GROUP):
            pivot = spread[i][i:i + 1, :]
            pivots = jnp.where(narrow_row == i, jnp.broadcast_to(pivot, pivots.shape), pivots)
            if i + 1 == GROUP:
                break
            scale = jnp.where(narrow_row > i, spread[i], 0.0) * (1.0 / pivot)
            for later in range(i + 1, GROUP):
                spread[later] = spread[later] - scale * spread[later][i:i + 1, :]
            left = left - scale * left[i:i + 1, :]
            right = right - scale * right[i:i + 1, :]
        root = 1.0 / jnp.sqrt(pivots)
        left, right = left * root, right * root
        inv_ref[start:start + GROUP, :] = right
        if start + GROUP < TILE:
            rest = jnp.where(lane_of >= start + GROUP, left, 0.0)
            both = jnp.concatenate([left, right], axis=1)
            work_ref[...] = work_ref[...] - lax.dot_general(
                rest, both, (((0,), (0,)), ((), ())), precision=HI, preferred_element_type=jnp.float32
            )

def invert_blocks(mat_ref, work_ref, inv_ref, first, last):
    tiles = mat_ref.shape[0] // TILE
    eye = jnp.where(
        lax.broadcasted_iota(jnp.int32, (TILE, TILE), 0)
        == lax.broadcasted_iota(jnp.int32, (TILE, TILE), 1), 1.0, 0.0
    ).astype(jnp.float32)

    def step(k, carry):
        at = pl.multiple_of(k * TILE, TILE)
        work_ref[:, :TILE] = mat_ref[pl.ds(at, TILE), pl.ds(at, TILE)]
        work_ref[:, TILE:] = eye
        eliminate_tile(work_ref, inv_ref)
        mat_ref[pl.ds(at, TILE), pl.ds(at, TILE)] = eye
        mat_ref[pl.ds(at, TILE), :] = jnp.dot(
            inv_ref[...], mat_ref[pl.ds(at, TILE), :], precision=HI, preferred_element_type=jnp.float32
        )

        def update(i, inner):
            below = pl.multiple_of(i * TILE, TILE)
            mat_ref[pl.ds(below, TILE), pl.ds(at, TILE)] = jnp.zeros((TILE, TILE), jnp.float32)
            mat_ref[pl.ds(below, TILE), :] = mat_ref[pl.ds(below, TILE), :] - lax.dot_general(
                mat_ref[pl.ds(at, TILE), pl.ds(below, TILE)],
                mat_ref[pl.ds(at, TILE), :],
                (((0,), (0,)), ((), ())),
                precision=HI,
                preferred_element_type=jnp.float32,
            )
            return inner

        lax.fori_loop(k + 1, tiles, update, 0)
        return carry

    lax.fori_loop(first, last, step, 0)


def solve_kernel(
    gram_ref, rhs_ref, out_ref, mat_ref, work_ref, inv_ref, slots_ref, sum_ref, own_sem,
    part_send, part_recv, sum_send, sum_recv,
):
    row = lax.axis_index("row")
    size = gram_ref.shape[0]
    height = size // X_CHIPS
    barrier = pltpu.get_barrier_semaphore()
    for step in range(1, X_CHIPS):
        pl.semaphore_signal(barrier, inc=1, device_id={"row": (row + step) % X_CHIPS}, device_id_type=MESH)
    mat_ref[...] = gram_ref[...]
    pl.semaphore_wait(barrier, X_CHIPS - 1)

    def rows(of_row):
        return pl.ds(pl.multiple_of(of_row * height, 8), height)

    copies = []
    for step in range(1, X_CHIPS):
        peer = (row + step) % X_CHIPS
        copy = pltpu.make_async_remote_copy(
            src_ref=rhs_ref.at[rows(peer), :],
            dst_ref=slots_ref.at[row],
            send_sem=part_send.at[step],
            recv_sem=part_recv.at[step],
            device_id={"row": peer},
            device_id_type=MESH,
        )
        copy.start()
        copies.append(copy)
    own = pltpu.make_async_copy(rhs_ref.at[rows(row), :], slots_ref.at[row], own_sem)
    own.start()
    own.wait()
    invert_blocks(mat_ref, work_ref, inv_ref, 0, size // TILE // 2)
    for step in range(1, X_CHIPS):
        here = slots_ref.at[(row + X_CHIPS - step) % X_CHIPS]
        pltpu.make_async_copy(here, here, part_recv.at[step]).wait()
    total = slots_ref[0]
    for other in range(1, X_CHIPS):
        total = total + slots_ref[other]
    sum_ref[rows(row), :] = total
    for step in range(1, X_CHIPS):
        copy = pltpu.make_async_remote_copy(
            src_ref=sum_ref.at[rows(row), :],
            dst_ref=sum_ref.at[rows(row), :],
            send_sem=sum_send.at[step],
            recv_sem=sum_recv.at[step],
            device_id={"row": (row + step) % X_CHIPS},
            device_id_type=MESH,
        )
        copy.start()
        copies.append(copy)
    invert_blocks(mat_ref, work_ref, inv_ref, size // TILE // 2, size // TILE)
    for step in range(1, X_CHIPS):
        here = sum_ref.at[rows((row + X_CHIPS - step) % X_CHIPS), :]
        pltpu.make_async_copy(here, here, sum_recv.at[step]).wait()
    tile_row = (row * height + lax.broadcasted_iota(jnp.int32, (height, size), 0)) // TILE
    tile_col = lax.broadcasted_iota(jnp.int32, (height, size), 1) // TILE
    inverse = jnp.where(tile_col <= tile_row, mat_ref[rows(row), :], 0.0)
    out_ref[...] = jnp.dot(inverse, sum_ref[...], precision=HI, preferred_element_type=jnp.float32)
    for copy in copies:
        copy.wait_send()


def solve_rows(gram, rhs):
    size = gram.shape[0]
    height = size // X_CHIPS
    return pl.pallas_call(
        solve_kernel,
        out_shape=jax.ShapeDtypeStruct((height, rhs.shape[1]), jnp.float32),
        in_specs=[pl.BlockSpec(memory_space=pltpu.VMEM)] * 2,
        out_specs=pl.BlockSpec(memory_space=pltpu.VMEM),
        scratch_shapes=[
            pltpu.VMEM((size, size), jnp.float32),
            pltpu.VMEM((TILE, 2 * TILE), jnp.float32),
            pltpu.VMEM((TILE, TILE), jnp.float32),
            pltpu.VMEM((X_CHIPS, height, rhs.shape[1]), jnp.float32),
            pltpu.VMEM(rhs.shape, jnp.float32),
            pltpu.SemaphoreType.DMA,
            pltpu.SemaphoreType.DMA((X_CHIPS,)),
            pltpu.SemaphoreType.DMA((X_CHIPS,)),
            pltpu.SemaphoreType.DMA((X_CHIPS,)),
            pltpu.SemaphoreType.DMA((X_CHIPS,)),
        ],
        compiler_params=pltpu.CompilerParams(collective_id=2, has_side_effects=True),
        name="solve_rows",
    )(gram, rhs)


def ring_places():
    me = lax.axis_index("col")
    return me % 2, me // 2 // Z_CHIPS, (me // 2) % Z_CHIPS


def col_of(core, y, z):
    return (y * Z_CHIPS + z) * 2 + core


def relay_rings(piece, send_sems, recv_sems, fill=()):
    core, y, z = ring_places()
    sent = []

    def pass_on(slot, src_y, src_z, to):
        copy = pltpu.make_async_remote_copy(
            src_ref=piece(core, src_y, src_z),
            dst_ref=piece(core, src_y, src_z),
            send_sem=send_sems.at[slot],
            recv_sem=recv_sems.at[slot],
            device_id={"col": to},
            device_id_type=MESH,
        )
        copy.start()
        sent.append(copy)

    def arrived(slot, src_core, src_y, src_z):
        here = piece(src_core, src_y, src_z)
        pltpu.make_async_copy(here, here, recv_sems.at[slot]).wait()

    z_up, z_down = (z + 1) % Z_CHIPS, (z + Z_CHIPS - 1) % Z_CHIPS
    y_up, y_down = (y + 1) % Y_CHIPS, (y + Y_CHIPS - 1) % Y_CHIPS
    y_far = (y + 2) % Y_CHIPS
    twin = col_of(1 - core, y, z)
    slots_z, slots_up, slots_down, slots_far, slots_twin = 0, 8, 16, 24, 32
    order = [0, 1, 7, 2, 6, 3, 5, 4]

    def source(back):
        return (z + Z_CHIPS - back) % Z_CHIPS

    def spread_y(back):
        pass_on(slots_up + back, y, source(back), col_of(core, y_up, z))
        pass_on(slots_down + back, y, source(back), col_of(core, y_down, z))
        pass_on(slots_twin + back, y, source(back), twin)

    def spread_far(back):
        arrived(slots_up + back, core, y_down, source(back))
        if back % 2 == 0:
            pass_on(slots_far + back, y_down, source(back), col_of(core, y_up, z))
        pass_on(slots_twin + 8 + back, y_down, source(back), twin)
        arrived(slots_down + back, core, y_up, source(back))
        if back % 2 == 1:
            pass_on(slots_far + back, y_up, source(back), col_of(core, y_down, z))
        pass_on(slots_twin + 16 + back, y_up, source(back), twin)

    def spread_twin(back):
        arrived(slots_far + back, core, y_far, source(back))
        pass_on(slots_twin + 24 + back, y_far, source(back), twin)

    pass_on(slots_z + 1, y, z, col_of(core, y, z_up))
    pass_on(slots_z + 7, y, z, col_of(core, y, z_down))
    spread_y(0)
    for work in fill[:1]:
        work()
    for at, back in enumerate(order):
        if back:
            arrived(slots_z + back, core, y, source(back))
            if back < 4:
                pass_on(slots_z + back + 1, y, source(back), col_of(core, y, z_up))
            if back > 5:
                pass_on(slots_z + back - 1, y, source(back), col_of(core, y, z_down))
            spread_y(back)
        if at >= 2:
            spread_far(order[at - 2])
        if at >= 4:
            spread_twin(order[at - 4])
    for back in order[6:]:
        spread_far(back)
    for back in order[4:]:
        spread_twin(back)
    for work in fill[1:]:
        work()
    for back in order:
        for kind, src_y in enumerate((y, y_down, y_up, y_far)):
            arrived(slots_twin + 8 * kind + back, 1 - core, src_y, source(back))
    for copy in sent:
        copy.wait_send()


def lead_kernel(block_ref, out_ref, own_sem, scatter_send, scatter_recv, send_sems, recv_sems):
    core, y, z = ring_places()
    chip = y * Z_CHIPS + z
    chips = Y_CHIPS * Z_CHIPS
    height = block_ref.shape[0] // chips
    barrier = pltpu.get_barrier_semaphore()

    def greet(step, carry):
        other = (chip + step) % chips
        pl.semaphore_signal(barrier, inc=1, device_id={"col": other * 2 + core}, device_id_type=MESH)
        return carry

    lax.fori_loop(1, chips, greet, 0)
    pl.semaphore_signal(barrier, inc=1, device_id={"col": chip * 2 + 1 - core}, device_id_type=MESH)
    pl.semaphore_wait(barrier, chips)

    def rows(of_chip):
        return pl.ds(pl.multiple_of(of_chip * height, 8), height)

    def scatter_copy(half, to_chip, step):
        return pltpu.make_async_remote_copy(
            src_ref=block_ref.at[rows(to_chip), :],
            dst_ref=out_ref.at[core, half, rows(to_chip), :],
            send_sem=scatter_send.at[step],
            recv_sem=scatter_recv.at[half],
            device_id={"col": to_chip * 2 + core},
            device_id_type=MESH,
        )

    for half in range(HALVES):

        @pl.when(chip == half)
        def _():
            def push(step, carry):
                scatter_copy(half, (half + step) % chips, step).start()
                return carry

            lax.fori_loop(1, chips, push, 0)
            own = pltpu.make_async_copy(
                block_ref.at[rows(half), :], out_ref.at[core, half, rows(half), :], own_sem
            )
            own.start()
            own.wait()

    for half in range(HALVES):

        @pl.when(chip != half)
        def _():
            here = out_ref.at[core, half, rows(chip), :]
            pltpu.make_async_copy(here, here, scatter_recv.at[half]).wait()

    relay_rings(
        lambda of_core, of_y, of_z: out_ref.at[of_core, :, rows(of_y * Z_CHIPS + of_z), :],
        send_sems,
        recv_sems,
    )
    for half in range(HALVES):

        @pl.when(chip == half)
        def _():
            def drain(step, carry):
                scatter_copy(half, (half + step) % chips, step).wait_send()
                return carry

            lax.fori_loop(1, chips, drain, 0)


def gram_kernel(
    own_ref, panels_ref, block_ref, out_ref, rhs_ref, part_ref, slots_ref,
    own_sem, row_send, row_recv, send_sems, recv_sems,
):
    core, y, z = ring_places()
    row = lax.axis_index("row")
    height = own_ref.shape[1]
    barrier = pltpu.get_barrier_semaphore()
    for near in (
        col_of(core, y, (z + 1) % Z_CHIPS),
        col_of(core, y, (z + Z_CHIPS - 1) % Z_CHIPS),
        col_of(core, (y + 1) % Y_CHIPS, z),
        col_of(core, (y + Y_CHIPS - 1) % Y_CHIPS, z),
        col_of(1 - core, y, z),
    ):
        pl.semaphore_signal(barrier, inc=1, device_id={"col": near}, device_id_type=MESH)
    for step in range(1, X_CHIPS):
        pl.semaphore_signal(barrier, inc=1, device_id={"row": (row + step) % X_CHIPS}, device_id_type=MESH)

    def panel_dot(left_ref, j):
        return lax.dot_general(
            left_ref[...], panels_ref[j % 2, j // 2], (((0,), (0,)), ((), ())),
            precision=HI, preferred_element_type=jnp.float32,
        )

    def rhs_dot(j):
        rhs_ref[j * B:(j + 1) * B, :] = lax.dot_general(
            panels_ref[j % 2, j // 2], block_ref[...], (((0,), (0,)), ((), ())),
            precision=HI, preferred_element_type=jnp.float32,
        )

    for j in range(P_SIZE):
        part_ref[:, j * B:(j + 1) * B] = panel_dot(own_ref, j)
    pl.semaphore_wait(barrier, 5 + X_CHIPS - 1)
    copies = []
    for step in range(1, X_CHIPS):
        copy = pltpu.make_async_remote_copy(
            src_ref=part_ref,
            dst_ref=slots_ref.at[row],
            send_sem=row_send.at[step],
            recv_sem=row_recv.at[step],
            device_id={"row": (row + step) % X_CHIPS},
            device_id_type=MESH,
        )
        copy.start()
        copies.append(copy)
    own = pltpu.make_async_copy(part_ref, slots_ref.at[row], own_sem)
    own.start()
    own.wait()
    rhs_dot(0)
    rhs_dot(1)
    for step in range(1, X_CHIPS):
        here = slots_ref.at[(row + X_CHIPS - step) % X_CHIPS]
        pltpu.make_async_copy(here, here, row_recv.at[step]).wait()
    total = slots_ref[0]
    for other in range(1, X_CHIPS):
        total = total + slots_ref[other]

    def piece(of_core, of_y, of_z):
        first = pl.multiple_of((of_y * Z_CHIPS + of_z) * height, 8)
        return out_ref.at[of_core, pl.ds(first, height), :]

    piece(core, y, z)[...] = total
    relay_rings(piece, send_sems, recv_sems, (lambda: rhs_dot(2), lambda: rhs_dot(3)))
    for copy in copies:
        copy.wait_send()


def spread_lead(block):
    height, width = block.shape
    chips = Y_CHIPS * Z_CHIPS
    return pl.pallas_call(
        lead_kernel,
        out_shape=jax.ShapeDtypeStruct((2, HALVES, height, width), jnp.float32),
        in_specs=[pl.BlockSpec(memory_space=pltpu.VMEM)],
        out_specs=pl.BlockSpec(memory_space=pltpu.VMEM),
        scratch_shapes=[
            pltpu.SemaphoreType.DMA,
            pltpu.SemaphoreType.DMA((chips,)),
            pltpu.SemaphoreType.DMA((HALVES,)),
            pltpu.SemaphoreType.DMA((64,)),
            pltpu.SemaphoreType.DMA((64,)),
        ],
        compiler_params=pltpu.CompilerParams(collective_id=0, has_side_effects=True),
        name="spread_lead",
    )(block)


def sum_gram(own, panels, block):
    width = own.shape[1]
    lead = P_SIZE * B
    chips = Y_CHIPS * Z_CHIPS
    return pl.pallas_call(
        gram_kernel,
        out_shape=(
            jax.ShapeDtypeStruct((2, chips * width, lead), jnp.float32),
            jax.ShapeDtypeStruct((lead, B), jnp.float32),
        ),
        in_specs=[pl.BlockSpec(memory_space=pltpu.VMEM)] * 3,
        out_specs=[pl.BlockSpec(memory_space=pltpu.VMEM)] * 2,
        scratch_shapes=[
            pltpu.VMEM((width, lead), jnp.float32),
            pltpu.VMEM((X_CHIPS, width, lead), jnp.float32),
            pltpu.SemaphoreType.DMA,
            pltpu.SemaphoreType.DMA((X_CHIPS,)),
            pltpu.SemaphoreType.DMA((X_CHIPS,)),
            pltpu.SemaphoreType.DMA((64,)),
            pltpu.SemaphoreType.DMA((64,)),
        ],
        compiler_params=pltpu.CompilerParams(collective_id=1, has_side_effects=True),
        name="sum_gram",
    )(own, panels, block)


def on_device(r_slab, arc_rows, arc_blocks):
    n_col = 2 * Y_CHIPS * Z_CHIPS
    col_index = lax.axis_index("col")
    row_index = lax.axis_index("row")
    n_arcs, blocks_here = arc_blocks.shape
    lead = P_SIZE * B
    live = arc_blocks.astype(jnp.float32)
    masked = (arc_rows.reshape(n_arcs, ARC_ROWS, blocks_here, B) * live[:, None, :, None]).reshape(
        arc_rows.shape
    )
    stacked = jnp.concatenate([r_slab, masked], axis=0)
    panels = spread_lead(stacked)
    share = lead // n_col
    row_start = (col_index % 2) * (lead // 2) + (col_index // 2) * share
    block = row_start // B
    own = lax.dynamic_slice(
        panels, (block % 2, block // 2, 0, row_start % B), (1, 1, stacked.shape[0], share)
    )[0, 0]
    gram, rhs = sum_gram(own, panels, stacked)
    mine_out = solve_rows(gram.reshape(lead, lead), rhs)
    row_ids = row_index * B + lax.broadcasted_iota(jnp.int32, (B, B), 0)
    col_ids = col_index * B + lax.broadcasted_iota(jnp.int32, (B, B), 1)
    return jnp.where(col_ids >= row_ids, mine_out, jnp.zeros_like(mine_out))


def solution(mesh):
    return jax.shard_map(
        on_device,
        mesh=mesh,
        in_specs=(P("row", "col"), P("row", "col"), P("row", "col")),
        out_specs=P("row", "col"),
        check_vma=False,
    )
```

```python
import jax
import jax.numpy as jnp
from jax import lax
from jax.experimental import pallas as pl
from jax.experimental.pallas import tpu as pltpu
from jax.sharding import PartitionSpec as P

B = 256
P_SIZE = 4
ARC_ROWS = 128
HI = lax.Precision.HIGHEST
TILE = 128
GROUP = 16
X_CHIPS, Y_CHIPS, Z_CHIPS = 4, 4, 8
HALVES = 2
MESH = pl.DeviceIdType.MESH


def inner_dot(left, right):
    return lax.dot_general(left, right, (((0,), (0,)), ((), ())), precision=HI)


def plain_dot(left, right):
    return jnp.dot(left, right, precision=HI)


def eliminate_tile(work_ref, inv_ref):
    row_of = lax.broadcasted_iota(jnp.int32, (GROUP, 2 * TILE), 0)
    lane_of = lax.broadcasted_iota(jnp.int32, (GROUP, TILE), 1)
    narrow_row = row_of[:, :TILE]
    for start in range(0, TILE, GROUP):
        panel = work_ref[start:start + GROUP, :]
        spread = [
            jnp.broadcast_to(panel[:, start + i:start + i + 1], (GROUP, TILE)) for i in range(GROUP)
        ]
        left, right = panel[:, :TILE], panel[:, TILE:]
        pivots = jnp.ones((GROUP, TILE), jnp.float32)
        for i in range(GROUP):
            pivot = spread[i][i:i + 1, :]
            pivots = jnp.where(narrow_row == i, jnp.broadcast_to(pivot, pivots.shape), pivots)
            if i + 1 == GROUP:
                break
            scale = jnp.where(narrow_row > i, spread[i], 0.0) * (1.0 / pivot)
            for later in range(i + 1, GROUP):
                spread[later] = spread[later] - scale * spread[later][i:i + 1, :]
            left = left - scale * left[i:i + 1, :]
            right = right - scale * right[i:i + 1, :]
        root = 1.0 / jnp.sqrt(pivots)
        left, right = left * root, right * root
        inv_ref[start:start + GROUP, :] = right
        if start + GROUP < TILE:
            rest = jnp.where(lane_of >= start + GROUP, left, 0.0)
            both = jnp.concatenate([left, right], axis=1)
            work_ref[...] = work_ref[...] - lax.dot_general(
                rest, both, (((0,), (0,)), ((), ())), precision=HI, preferred_element_type=jnp.float32
            )

def invert_blocks(mat_ref, work_ref, inv_ref, first, last):
    tiles = mat_ref.shape[0] // TILE
    eye = jnp.where(
        lax.broadcasted_iota(jnp.int32, (TILE, TILE), 0)
        == lax.broadcasted_iota(jnp.int32, (TILE, TILE), 1), 1.0, 0.0
    ).astype(jnp.float32)

    def step(k, carry):
        at = pl.multiple_of(k * TILE, TILE)
        work_ref[:, :TILE] = mat_ref[pl.ds(at, TILE), pl.ds(at, TILE)]
        work_ref[:, TILE:] = eye
        eliminate_tile(work_ref, inv_ref)
        mat_ref[pl.ds(at, TILE), pl.ds(at, TILE)] = eye
        mat_ref[pl.ds(at, TILE), :] = jnp.dot(
            inv_ref[...], mat_ref[pl.ds(at, TILE), :], precision=HI, preferred_element_type=jnp.float32
        )

        def update(i, inner):
            below = pl.multiple_of(i * TILE, TILE)
            mat_ref[pl.ds(below, TILE), pl.ds(at, TILE)] = jnp.zeros((TILE, TILE), jnp.float32)
            mat_ref[pl.ds(below, TILE), :] = mat_ref[pl.ds(below, TILE), :] - lax.dot_general(
                mat_ref[pl.ds(at, TILE), pl.ds(below, TILE)],
                mat_ref[pl.ds(at, TILE), :],
                (((0,), (0,)), ((), ())),
                precision=HI,
                preferred_element_type=jnp.float32,
            )
            return inner

        lax.fori_loop(k + 1, tiles, update, 0)
        return carry

    lax.fori_loop(first, last, step, 0)


def solve_kernel(
    gram_ref, rhs_ref, out_ref, mat_ref, work_ref, inv_ref, slots_ref, sum_ref, own_sem,
    part_send, part_recv, sum_send, sum_recv,
):
    row = lax.axis_index("row")
    size = gram_ref.shape[0]
    height = size // X_CHIPS
    barrier = pltpu.get_barrier_semaphore()
    for step in range(1, X_CHIPS):
        pl.semaphore_signal(barrier, inc=1, device_id={"row": (row + step) % X_CHIPS}, device_id_type=MESH)
    mat_ref[...] = gram_ref[...]
    pl.semaphore_wait(barrier, X_CHIPS - 1)

    def rows(of_row):
        return pl.ds(pl.multiple_of(of_row * height, 8), height)

    copies = []
    for step in range(1, X_CHIPS):
        peer = (row + step) % X_CHIPS
        copy = pltpu.make_async_remote_copy(
            src_ref=rhs_ref.at[rows(peer), :],
            dst_ref=slots_ref.at[row],
            send_sem=part_send.at[step],
            recv_sem=part_recv.at[step],
            device_id={"row": peer},
            device_id_type=MESH,
        )
        copy.start()
        copies.append(copy)
    own = pltpu.make_async_copy(rhs_ref.at[rows(row), :], slots_ref.at[row], own_sem)
    own.start()
    own.wait()
    invert_blocks(mat_ref, work_ref, inv_ref, 0, size // TILE // 2)
    for step in range(1, X_CHIPS):
        here = slots_ref.at[(row + X_CHIPS - step) % X_CHIPS]
        pltpu.make_async_copy(here, here, part_recv.at[step]).wait()
    total = slots_ref[0]
    for other in range(1, X_CHIPS):
        total = total + slots_ref[other]
    sum_ref[rows(row), :] = total
    for step in range(1, X_CHIPS):
        copy = pltpu.make_async_remote_copy(
            src_ref=sum_ref.at[rows(row), :],
            dst_ref=sum_ref.at[rows(row), :],
            send_sem=sum_send.at[step],
            recv_sem=sum_recv.at[step],
            device_id={"row": (row + step) % X_CHIPS},
            device_id_type=MESH,
        )
        copy.start()
        copies.append(copy)
    invert_blocks(mat_ref, work_ref, inv_ref, size // TILE // 2, size // TILE)
    for step in range(1, X_CHIPS):
        here = sum_ref.at[rows((row + X_CHIPS - step) % X_CHIPS), :]
        pltpu.make_async_copy(here, here, sum_recv.at[step]).wait()
    tile_row = (row * height + lax.broadcasted_iota(jnp.int32, (height, size), 0)) // TILE
    tile_col = lax.broadcasted_iota(jnp.int32, (height, size), 1) // TILE
    inverse = jnp.where(tile_col <= tile_row, mat_ref[rows(row), :], 0.0)
    out_ref[...] = jnp.dot(inverse, sum_ref[...], precision=HI, preferred_element_type=jnp.float32)
    for copy in copies:
        copy.wait_send()


def solve_rows(gram, rhs):
    size = gram.shape[0]
    height = size // X_CHIPS
    return pl.pallas_call(
        solve_kernel,
        out_shape=jax.ShapeDtypeStruct((height, rhs.shape[1]), jnp.float32),
        in_specs=[pl.BlockSpec(memory_space=pltpu.VMEM)] * 2,
        out_specs=pl.BlockSpec(memory_space=pltpu.VMEM),
        scratch_shapes=[
            pltpu.VMEM((size, size), jnp.float32),
            pltpu.VMEM((TILE, 2 * TILE), jnp.float32),
            pltpu.VMEM((TILE, TILE), jnp.float32),
            pltpu.VMEM((X_CHIPS, height, rhs.shape[1]), jnp.float32),
            pltpu.VMEM(rhs.shape, jnp.float32),
            pltpu.SemaphoreType.DMA,
            pltpu.SemaphoreType.DMA((X_CHIPS,)),
            pltpu.SemaphoreType.DMA((X_CHIPS,)),
            pltpu.SemaphoreType.DMA((X_CHIPS,)),
            pltpu.SemaphoreType.DMA((X_CHIPS,)),
        ],
        compiler_params=pltpu.CompilerParams(collective_id=2, has_side_effects=True),
        name="solve_rows",
    )(gram, rhs)


def ring_places():
    me = lax.axis_index("col")
    return me % 2, me // 2 // Z_CHIPS, (me // 2) % Z_CHIPS


def col_of(core, y, z):
    return (y * Z_CHIPS + z) * 2 + core


def relay_rings(piece, send_sems, recv_sems, fill=()):
    core, y, z = ring_places()
    sent = []

    def pass_on(slot, src_y, src_z, to):
        copy = pltpu.make_async_remote_copy(
            src_ref=piece(core, src_y, src_z),
            dst_ref=piece(core, src_y, src_z),
            send_sem=send_sems.at[slot],
            recv_sem=recv_sems.at[slot],
            device_id={"col": to},
            device_id_type=MESH,
        )
        copy.start()
        sent.append(copy)

    def arrived(slot, src_core, src_y, src_z):
        here = piece(src_core, src_y, src_z)
        pltpu.make_async_copy(here, here, recv_sems.at[slot]).wait()

    z_up, z_down = (z + 1) % Z_CHIPS, (z + Z_CHIPS - 1) % Z_CHIPS
    y_up, y_down = (y + 1) % Y_CHIPS, (y + Y_CHIPS - 1) % Y_CHIPS
    y_far = (y + 2) % Y_CHIPS
    twin = col_of(1 - core, y, z)
    slots_z, slots_up, slots_down, slots_far, slots_twin = 0, 8, 16, 24, 32
    order = [0, 1, 7, 2, 6, 3, 5, 4]

    def source(back):
        return (z + Z_CHIPS - back) % Z_CHIPS

    def spread_y(back):
        pass_on(slots_up + back, y, source(back), col_of(core, y_up, z))
        pass_on(slots_down + back, y, source(back), col_of(core, y_down, z))
        pass_on(slots_twin + back, y, source(back), twin)

    def spread_far(back):
        arrived(slots_up + back, core, y_down, source(back))
        if back % 2 == 0:
            pass_on(slots_far + back, y_down, source(back), col_of(core, y_up, z))
        pass_on(slots_twin + 8 + back, y_down, source(back), twin)
        arrived(slots_down + back, core, y_up, source(back))
        if back % 2 == 1:
            pass_on(slots_far + back, y_up, source(back), col_of(core, y_down, z))
        pass_on(slots_twin + 16 + back, y_up, source(back), twin)

    def spread_twin(back):
        arrived(slots_far + back, core, y_far, source(back))
        pass_on(slots_twin + 24 + back, y_far, source(back), twin)

    pass_on(slots_z + 1, y, z, col_of(core, y, z_up))
    pass_on(slots_z + 7, y, z, col_of(core, y, z_down))
    spread_y(0)
    for work in fill[:1]:
        work()
    for at, back in enumerate(order):
        if back:
            arrived(slots_z + back, core, y, source(back))
            if back < 4:
                pass_on(slots_z + back + 1, y, source(back), col_of(core, y, z_up))
            if back > 5:
                pass_on(slots_z + back - 1, y, source(back), col_of(core, y, z_down))
            spread_y(back)
        if at >= 2:
            spread_far(order[at - 2])
        if at >= 4:
            spread_twin(order[at - 4])
    for back in order[6:]:
        spread_far(back)
    for back in order[4:]:
        spread_twin(back)
    for work in fill[1:]:
        work()
    for back in order:
        for kind, src_y in enumerate((y, y_down, y_up, y_far)):
            arrived(slots_twin + 8 * kind + back, 1 - core, src_y, source(back))
    for copy in sent:
        copy.wait_send()


def lead_kernel(
    block_ref, out_ref, pass_ref, far_ref, own_sem, out_send, direct_recv, pass_recv, far_recv,
    pass_send, far_send, send_sems, recv_sems,
):
    core, y, z = ring_places()
    chip = y * Z_CHIPS + z
    chips = Y_CHIPS * Z_CHIPS
    height = block_ref.shape[0] // chips
    barrier = pltpu.get_barrier_semaphore()

    def greet(step, carry):
        other = (chip + step) % chips
        pl.semaphore_signal(barrier, inc=1, device_id={"col": other * 2 + core}, device_id_type=MESH)
        return carry

    lax.fori_loop(1, chips, greet, 0)
    pl.semaphore_signal(barrier, inc=1, device_id={"col": chip * 2 + 1 - core}, device_id_type=MESH)
    pl.semaphore_wait(barrier, chips)

    def rows(of_chip):
        return pl.ds(pl.multiple_of(of_chip * height, 8), height)

    def send(source, target, send_sem, recv_sem, to_y, to_z):
        copy = pltpu.make_async_remote_copy(
            src_ref=source, dst_ref=target, send_sem=send_sem, recv_sem=recv_sem,
            device_id={"col": col_of(core, to_y, to_z)}, device_id_type=MESH,
        )
        copy.start()
        return copy

    def arrived(here, sem):
        pltpu.make_async_copy(here, here, sem).wait()

    ahead = (4, 3, 5, 2, 6, 1, 7)
    for half in range(HALVES):

        def place(of_y, step):
            return of_y * Z_CHIPS + (half + step) % Z_CHIPS

        def final(of_y, step):
            return out_ref.at[core, half, rows(place(of_y, step)), :]

        @pl.when((z == half) & (y == 0))
        def _():
            copies = []

            def push(source, target, recv_sem, to_y, to_z):
                copies.append(send(source, target, out_send.at[len(copies)], recv_sem, to_y, to_z))

            def held(of_y, step):
                return block_ref.at[rows(place(of_y, step)), :]

            for step in ahead:
                via, slot = (1, step // 2) if step % 2 else (3, step // 2)
                push(held(2, step), far_ref.at[slot], far_recv.at[slot], via, half)
                for to_y in (1, 3):
                    push(held(to_y, step), pass_ref.at[step], pass_recv.at[step], to_y, half)
                to_z = (half + step) % Z_CHIPS
                push(held(0, step), final(0, step), direct_recv.at[half], 0, to_z)
            for to_y in (2, 1, 3):
                push(held(to_y, 0), final(to_y, 0), direct_recv.at[half], to_y, half)
            own = pltpu.make_async_copy(held(0, 0), final(0, 0), own_sem)
            own.start()
            own.wait()
            for copy in copies:
                copy.wait_send()

        @pl.when((z == half) & (y != 0))
        def _():
            copies = []
            for step in ahead:
                for via in (1, 3):
                    if step % 2 == (via == 1):

                        @pl.when(y == via)
                        def _():
                            slot = step // 2
                            arrived(far_ref.at[slot], far_recv.at[slot])
                            send(
                                far_ref.at[slot], pass_ref.at[step], far_send.at[slot],
                                pass_recv.at[step], 2, half,
                            )

                arrived(pass_ref.at[step], pass_recv.at[step])
                copies.append(
                    send(
                        pass_ref.at[step], final(y, step), pass_send.at[step],
                        direct_recv.at[half], y, (half + step) % Z_CHIPS,
                    )
                )
            for copy in copies:
                copy.wait_send()
            for step in ahead:
                for via in (1, 3):
                    if step % 2 == (via == 1):

                        @pl.when(y == via)
                        def _():
                            slot = step // 2
                            arrived(far_ref.at[slot], far_send.at[slot])

    for half in range(HALVES):

        @pl.when(chip != half)
        def _():
            arrived(out_ref.at[core, half, rows(chip), :], direct_recv.at[half])

    relay_rings(
        lambda of_core, of_y, of_z: out_ref.at[of_core, :, rows(of_y * Z_CHIPS + of_z), :],
        send_sems,
        recv_sems,
    )


def gram_kernel(
    own_ref, panels_ref, block_ref, out_ref, rhs_ref, part_ref, slots_ref,
    own_sem, row_send, row_recv, send_sems, recv_sems,
):
    core, y, z = ring_places()
    row = lax.axis_index("row")
    height = own_ref.shape[1]
    barrier = pltpu.get_barrier_semaphore()
    for near in (
        col_of(core, y, (z + 1) % Z_CHIPS),
        col_of(core, y, (z + Z_CHIPS - 1) % Z_CHIPS),
        col_of(core, (y + 1) % Y_CHIPS, z),
        col_of(core, (y + Y_CHIPS - 1) % Y_CHIPS, z),
        col_of(1 - core, y, z),
    ):
        pl.semaphore_signal(barrier, inc=1, device_id={"col": near}, device_id_type=MESH)
    for step in range(1, X_CHIPS):
        pl.semaphore_signal(barrier, inc=1, device_id={"row": (row + step) % X_CHIPS}, device_id_type=MESH)

    def panel_dot(left_ref, j):
        return lax.dot_general(
            left_ref[...], panels_ref[j % 2, j // 2], (((0,), (0,)), ((), ())),
            precision=HI, preferred_element_type=jnp.float32,
        )

    def rhs_dot(j):
        rhs_ref[j * B:(j + 1) * B, :] = lax.dot_general(
            panels_ref[j % 2, j // 2], block_ref[...], (((0,), (0,)), ((), ())),
            precision=HI, preferred_element_type=jnp.float32,
        )

    for j in range(P_SIZE):
        part_ref[:, j * B:(j + 1) * B] = panel_dot(own_ref, j)
    pl.semaphore_wait(barrier, 5 + X_CHIPS - 1)
    copies = []
    for step in range(1, X_CHIPS):
        copy = pltpu.make_async_remote_copy(
            src_ref=part_ref,
            dst_ref=slots_ref.at[row],
            send_sem=row_send.at[step],
            recv_sem=row_recv.at[step],
            device_id={"row": (row + step) % X_CHIPS},
            device_id_type=MESH,
        )
        copy.start()
        copies.append(copy)
    own = pltpu.make_async_copy(part_ref, slots_ref.at[row], own_sem)
    own.start()
    own.wait()
    rhs_dot(0)
    rhs_dot(1)
    for step in range(1, X_CHIPS):
        here = slots_ref.at[(row + X_CHIPS - step) % X_CHIPS]
        pltpu.make_async_copy(here, here, row_recv.at[step]).wait()
    total = slots_ref[0]
    for other in range(1, X_CHIPS):
        total = total + slots_ref[other]

    def piece(of_core, of_y, of_z):
        first = pl.multiple_of((of_y * Z_CHIPS + of_z) * height, 8)
        return out_ref.at[of_core, pl.ds(first, height), :]

    piece(core, y, z)[...] = total
    relay_rings(piece, send_sems, recv_sems, (lambda: rhs_dot(2), lambda: rhs_dot(3)))
    for copy in copies:
        copy.wait_send()


def spread_lead(block):
    height, width = block.shape
    chips = Y_CHIPS * Z_CHIPS
    return pl.pallas_call(
        lead_kernel,
        out_shape=jax.ShapeDtypeStruct((2, HALVES, height, width), jnp.float32),
        in_specs=[pl.BlockSpec(memory_space=pltpu.VMEM)],
        out_specs=pl.BlockSpec(memory_space=pltpu.VMEM),
        scratch_shapes=[
            pltpu.VMEM((Z_CHIPS, height // chips, width), jnp.float32),
            pltpu.VMEM((4, height // chips, width), jnp.float32),
            pltpu.SemaphoreType.DMA,
            pltpu.SemaphoreType.DMA((chips,)),
            pltpu.SemaphoreType.DMA((HALVES,)),
            pltpu.SemaphoreType.DMA((Z_CHIPS,)),
            pltpu.SemaphoreType.DMA((4,)),
            pltpu.SemaphoreType.DMA((Z_CHIPS,)),
            pltpu.SemaphoreType.DMA((4,)),
            pltpu.SemaphoreType.DMA((64,)),
            pltpu.SemaphoreType.DMA((64,)),
        ],
        compiler_params=pltpu.CompilerParams(collective_id=0, has_side_effects=True),
        name="spread_lead",
    )(block)


def sum_gram(own, panels, block):
    width = own.shape[1]
    lead = P_SIZE * B
    chips = Y_CHIPS * Z_CHIPS
    return pl.pallas_call(
        gram_kernel,
        out_shape=(
            jax.ShapeDtypeStruct((2, chips * width, lead), jnp.float32),
            jax.ShapeDtypeStruct((lead, B), jnp.float32),
        ),
        in_specs=[pl.BlockSpec(memory_space=pltpu.VMEM)] * 3,
        out_specs=[pl.BlockSpec(memory_space=pltpu.VMEM)] * 2,
        scratch_shapes=[
            pltpu.VMEM((width, lead), jnp.float32),
            pltpu.VMEM((X_CHIPS, width, lead), jnp.float32),
            pltpu.SemaphoreType.DMA,
            pltpu.SemaphoreType.DMA((X_CHIPS,)),
            pltpu.SemaphoreType.DMA((X_CHIPS,)),
            pltpu.SemaphoreType.DMA((64,)),
            pltpu.SemaphoreType.DMA((64,)),
        ],
        compiler_params=pltpu.CompilerParams(collective_id=1, has_side_effects=True),
        name="sum_gram",
    )(own, panels, block)


def on_device(r_slab, arc_rows, arc_blocks):
    n_col = 2 * Y_CHIPS * Z_CHIPS
    col_index = lax.axis_index("col")
    row_index = lax.axis_index("row")
    n_arcs, blocks_here = arc_blocks.shape
    lead = P_SIZE * B
    live = arc_blocks.astype(jnp.float32)
    masked = (arc_rows.reshape(n_arcs, ARC_ROWS, blocks_here, B) * live[:, None, :, None]).reshape(
        arc_rows.shape
    )
    stacked = jnp.concatenate([r_slab, masked], axis=0)
    panels = spread_lead(stacked)
    share = lead // n_col
    row_start = (col_index % 2) * (lead // 2) + (col_index // 2) * share
    block = row_start // B
    own = lax.dynamic_slice(
        panels, (block % 2, block // 2, 0, row_start % B), (1, 1, stacked.shape[0], share)
    )[0, 0]
    gram, rhs = sum_gram(own, panels, stacked)
    mine_out = solve_rows(gram.reshape(lead, lead), rhs)
    row_ids = row_index * B + lax.broadcasted_iota(jnp.int32, (B, B), 0)
    col_ids = col_index * B + lax.broadcasted_iota(jnp.int32, (B, B), 1)
    return jnp.where(col_ids >= row_ids, mine_out, jnp.zeros_like(mine_out))


def solution(mesh):
    return jax.shard_map(
        on_device,
        mesh=mesh,
        in_specs=(P("row", "col"), P("row", "col"), P("row", "col")),
        out_specs=P("row", "col"),
        check_vma=False,
    )
```

```python
import jax
import jax.numpy as jnp
from jax import lax
from jax.experimental import pallas as pl
from jax.experimental.pallas import tpu as pltpu
from jax.sharding import PartitionSpec as P

B = 256
P_SIZE = 4
ARC_ROWS = 128
HI = lax.Precision.HIGHEST
TILE = 128
GROUP = 32
X_CHIPS, Y_CHIPS, Z_CHIPS = 4, 4, 8
HALVES = 2
MESH = pl.DeviceIdType.MESH


def inner_dot(left, right):
    return lax.dot_general(left, right, (((0,), (0,)), ((), ())), precision=HI)


def plain_dot(left, right):
    return jnp.dot(left, right, precision=HI)


def eliminate_tile(work_ref, inv_ref):
    row_of = lax.broadcasted_iota(jnp.int32, (GROUP, 2 * TILE), 0)
    lane_of = lax.broadcasted_iota(jnp.int32, (GROUP, TILE), 1)
    narrow_row = row_of[:, :TILE]
    for start in range(0, TILE, GROUP):
        panel = work_ref[start:start + GROUP, :]
        spread = [
            jnp.broadcast_to(panel[:, start + i:start + i + 1], (GROUP, TILE)) for i in range(GROUP)
        ]
        left, right = panel[:, :TILE], panel[:, TILE:]
        pivots = jnp.ones((GROUP, TILE), jnp.float32)
        for i in range(GROUP):
            pivot = spread[i][i:i + 1, :]
            pivots = jnp.where(narrow_row == i, jnp.broadcast_to(pivot, pivots.shape), pivots)
            if i + 1 == GROUP:
                break
            scale = jnp.where(narrow_row > i, spread[i], 0.0) * (1.0 / pivot)
            for later in range(i + 1, GROUP):
                spread[later] = spread[later] - scale * spread[later][i:i + 1, :]
            left = left - scale * left[i:i + 1, :]
            right = right - scale * right[i:i + 1, :]
        root = 1.0 / jnp.sqrt(pivots)
        left, right = left * root, right * root
        inv_ref[start:start + GROUP, :] = right
        if start + GROUP < TILE:
            rest = jnp.where(lane_of >= start + GROUP, left, 0.0)
            both = jnp.concatenate([left, right], axis=1)
            work_ref[...] = work_ref[...] - lax.dot_general(
                rest, both, (((0,), (0,)), ((), ())), precision=HI, preferred_element_type=jnp.float32
            )

def invert_blocks(mat_ref, work_ref, inv_ref, first, last):
    tiles = mat_ref.shape[0] // TILE
    eye = jnp.where(
        lax.broadcasted_iota(jnp.int32, (TILE, TILE), 0)
        == lax.broadcasted_iota(jnp.int32, (TILE, TILE), 1), 1.0, 0.0
    ).astype(jnp.float32)

    def step(k, carry):
        at = pl.multiple_of(k * TILE, TILE)
        work_ref[:, :TILE] = mat_ref[pl.ds(at, TILE), pl.ds(at, TILE)]
        work_ref[:, TILE:] = eye
        eliminate_tile(work_ref, inv_ref)
        mat_ref[pl.ds(at, TILE), pl.ds(at, TILE)] = eye
        mat_ref[pl.ds(at, TILE), :] = jnp.dot(
            inv_ref[...], mat_ref[pl.ds(at, TILE), :], precision=HI, preferred_element_type=jnp.float32
        )

        def update(i, inner):
            below = pl.multiple_of(i * TILE, TILE)
            mat_ref[pl.ds(below, TILE), pl.ds(at, TILE)] = jnp.zeros((TILE, TILE), jnp.float32)
            mat_ref[pl.ds(below, TILE), :] = mat_ref[pl.ds(below, TILE), :] - lax.dot_general(
                mat_ref[pl.ds(at, TILE), pl.ds(below, TILE)],
                mat_ref[pl.ds(at, TILE), :],
                (((0,), (0,)), ((), ())),
                precision=HI,
                preferred_element_type=jnp.float32,
            )
            return inner

        lax.fori_loop(k + 1, tiles, update, 0)
        return carry

    lax.fori_loop(first, last, step, 0)


def solve_kernel(
    gram_ref, rhs_ref, out_ref, mat_ref, work_ref, inv_ref, slots_ref, sum_ref, own_sem,
    part_send, part_recv, sum_send, sum_recv,
):
    row = lax.axis_index("row")
    size = gram_ref.shape[0]
    height = size // X_CHIPS
    barrier = pltpu.get_barrier_semaphore()
    for step in range(1, X_CHIPS):
        pl.semaphore_signal(barrier, inc=1, device_id={"row": (row + step) % X_CHIPS}, device_id_type=MESH)
    mat_ref[...] = gram_ref[...]
    pl.semaphore_wait(barrier, X_CHIPS - 1)

    def rows(of_row):
        return pl.ds(pl.multiple_of(of_row * height, 8), height)

    copies = []
    for step in range(1, X_CHIPS):
        peer = (row + step) % X_CHIPS
        copy = pltpu.make_async_remote_copy(
            src_ref=rhs_ref.at[rows(peer), :],
            dst_ref=slots_ref.at[row],
            send_sem=part_send.at[step],
            recv_sem=part_recv.at[step],
            device_id={"row": peer},
            device_id_type=MESH,
        )
        copy.start()
        copies.append(copy)
    own = pltpu.make_async_copy(rhs_ref.at[rows(row), :], slots_ref.at[row], own_sem)
    own.start()
    own.wait()
    invert_blocks(mat_ref, work_ref, inv_ref, 0, size // TILE // 2)
    for step in range(1, X_CHIPS):
        here = slots_ref.at[(row + X_CHIPS - step) % X_CHIPS]
        pltpu.make_async_copy(here, here, part_recv.at[step]).wait()
    total = slots_ref[0]
    for other in range(1, X_CHIPS):
        total = total + slots_ref[other]
    sum_ref[rows(row), :] = total
    for step in range(1, X_CHIPS):
        copy = pltpu.make_async_remote_copy(
            src_ref=sum_ref.at[rows(row), :],
            dst_ref=sum_ref.at[rows(row), :],
            send_sem=sum_send.at[step],
            recv_sem=sum_recv.at[step],
            device_id={"row": (row + step) % X_CHIPS},
            device_id_type=MESH,
        )
        copy.start()
        copies.append(copy)
    invert_blocks(mat_ref, work_ref, inv_ref, size // TILE // 2, size // TILE)
    for step in range(1, X_CHIPS):
        here = sum_ref.at[rows((row + X_CHIPS - step) % X_CHIPS), :]
        pltpu.make_async_copy(here, here, sum_recv.at[step]).wait()
    tile_row = (row * height + lax.broadcasted_iota(jnp.int32, (height, size), 0)) // TILE
    tile_col = lax.broadcasted_iota(jnp.int32, (height, size), 1) // TILE
    inverse = jnp.where(tile_col <= tile_row, mat_ref[rows(row), :], 0.0)
    out_ref[...] = jnp.dot(inverse, sum_ref[...], precision=HI, preferred_element_type=jnp.float32)
    for copy in copies:
        copy.wait_send()


def solve_rows(gram, rhs):
    size = gram.shape[0]
    height = size // X_CHIPS
    return pl.pallas_call(
        solve_kernel,
        out_shape=jax.ShapeDtypeStruct((height, rhs.shape[1]), jnp.float32),
        in_specs=[pl.BlockSpec(memory_space=pltpu.VMEM)] * 2,
        out_specs=pl.BlockSpec(memory_space=pltpu.VMEM),
        scratch_shapes=[
            pltpu.VMEM((size, size), jnp.float32),
            pltpu.VMEM((TILE, 2 * TILE), jnp.float32),
            pltpu.VMEM((TILE, TILE), jnp.float32),
            pltpu.VMEM((X_CHIPS, height, rhs.shape[1]), jnp.float32),
            pltpu.VMEM(rhs.shape, jnp.float32),
            pltpu.SemaphoreType.DMA,
            pltpu.SemaphoreType.DMA((X_CHIPS,)),
            pltpu.SemaphoreType.DMA((X_CHIPS,)),
            pltpu.SemaphoreType.DMA((X_CHIPS,)),
            pltpu.SemaphoreType.DMA((X_CHIPS,)),
        ],
        compiler_params=pltpu.CompilerParams(collective_id=2, has_side_effects=True),
        name="solve_rows",
    )(gram, rhs)


def ring_places():
    me = lax.axis_index("col")
    return me % 2, me // 2 // Z_CHIPS, (me // 2) % Z_CHIPS


def col_of(core, y, z):
    return (y * Z_CHIPS + z) * 2 + core


def relay_rings(piece, send_sems, recv_sems, fill=()):
    core, y, z = ring_places()
    sent = []

    def pass_on(slot, src_y, src_z, to):
        copy = pltpu.make_async_remote_copy(
            src_ref=piece(core, src_y, src_z),
            dst_ref=piece(core, src_y, src_z),
            send_sem=send_sems.at[slot],
            recv_sem=recv_sems.at[slot],
            device_id={"col": to},
            device_id_type=MESH,
        )
        copy.start()
        sent.append(copy)

    def arrived(slot, src_core, src_y, src_z):
        here = piece(src_core, src_y, src_z)
        pltpu.make_async_copy(here, here, recv_sems.at[slot]).wait()

    z_up, z_down = (z + 1) % Z_CHIPS, (z + Z_CHIPS - 1) % Z_CHIPS
    y_up, y_down = (y + 1) % Y_CHIPS, (y + Y_CHIPS - 1) % Y_CHIPS
    y_far = (y + 2) % Y_CHIPS
    twin = col_of(1 - core, y, z)
    slots_z, slots_up, slots_down, slots_far, slots_twin = 0, 8, 16, 24, 32
    order = [0, 1, 7, 2, 6, 3, 5, 4]

    def source(back):
        return (z + Z_CHIPS - back) % Z_CHIPS

    def spread_y(back):
        pass_on(slots_up + back, y, source(back), col_of(core, y_up, z))
        pass_on(slots_down + back, y, source(back), col_of(core, y_down, z))
        pass_on(slots_twin + back, y, source(back), twin)

    def spread_far(back):
        arrived(slots_up + back, core, y_down, source(back))
        if back % 2 == 0:
            pass_on(slots_far + back, y_down, source(back), col_of(core, y_up, z))
        pass_on(slots_twin + 8 + back, y_down, source(back), twin)
        arrived(slots_down + back, core, y_up, source(back))
        if back % 2 == 1:
            pass_on(slots_far + back, y_up, source(back), col_of(core, y_down, z))
        pass_on(slots_twin + 16 + back, y_up, source(back), twin)

    def spread_twin(back):
        arrived(slots_far + back, core, y_far, source(back))
        pass_on(slots_twin + 24 + back, y_far, source(back), twin)

    pass_on(slots_z + 1, y, z, col_of(core, y, z_up))
    pass_on(slots_z + 7, y, z, col_of(core, y, z_down))
    spread_y(0)
    for work in fill[:1]:
        work()
    for at, back in enumerate(order):
        if back:
            arrived(slots_z + back, core, y, source(back))
            if back < 4:
                pass_on(slots_z + back + 1, y, source(back), col_of(core, y, z_up))
            if back > 5:
                pass_on(slots_z + back - 1, y, source(back), col_of(core, y, z_down))
            spread_y(back)
        if at >= 2:
            spread_far(order[at - 2])
        if at >= 4:
            spread_twin(order[at - 4])
    for back in order[6:]:
        spread_far(back)
    for back in order[4:]:
        spread_twin(back)
    for work in fill[1:]:
        work()
    for back in order:
        for kind, src_y in enumerate((y, y_down, y_up, y_far)):
            arrived(slots_twin + 8 * kind + back, 1 - core, src_y, source(back))
    for copy in sent:
        copy.wait_send()


def lead_kernel(
    block_ref, out_ref, pass_ref, far_ref, own_sem, out_send, direct_recv, pass_recv, far_recv,
    pass_send, far_send, send_sems, recv_sems,
):
    core, y, z = ring_places()
    chip = y * Z_CHIPS + z
    chips = Y_CHIPS * Z_CHIPS
    height = block_ref.shape[0] // chips
    barrier = pltpu.get_barrier_semaphore()

    def greet(step, carry):
        other = (chip + step) % chips
        pl.semaphore_signal(barrier, inc=1, device_id={"col": other * 2 + core}, device_id_type=MESH)
        return carry

    lax.fori_loop(1, chips, greet, 0)
    pl.semaphore_signal(barrier, inc=1, device_id={"col": chip * 2 + 1 - core}, device_id_type=MESH)
    pl.semaphore_wait(barrier, chips)

    def rows(of_chip):
        return pl.ds(pl.multiple_of(of_chip * height, 8), height)

    def send(source, target, send_sem, recv_sem, to_y, to_z):
        copy = pltpu.make_async_remote_copy(
            src_ref=source, dst_ref=target, send_sem=send_sem, recv_sem=recv_sem,
            device_id={"col": col_of(core, to_y, to_z)}, device_id_type=MESH,
        )
        copy.start()
        return copy

    def arrived(here, sem):
        pltpu.make_async_copy(here, here, sem).wait()

    ahead = (4, 3, 5, 2, 6, 1, 7)
    for half in range(HALVES):

        def place(of_y, step):
            return of_y * Z_CHIPS + (half + step) % Z_CHIPS

        def final(of_y, step):
            return out_ref.at[core, half, rows(place(of_y, step)), :]

        @pl.when((z == half) & (y == 0))
        def _():
            slots = iter(range(chips))

            def push(source, target, recv_sem, to_y, to_z):
                send(source, target, out_send.at[next(slots)], recv_sem, to_y, to_z)

            def held(of_y, step):
                return block_ref.at[rows(place(of_y, step)), :]

            for step in ahead:
                via, slot = (1, step // 2) if step % 2 else (3, step // 2)
                push(held(2, step), far_ref.at[slot], far_recv.at[slot], via, half)
                for to_y in (1, 3):
                    push(held(to_y, step), pass_ref.at[step], pass_recv.at[step], to_y, half)
                to_z = (half + step) % Z_CHIPS
                push(held(0, step), final(0, step), direct_recv.at[half], 0, to_z)
            for to_y in (2, 1, 3):
                push(held(to_y, 0), final(to_y, 0), direct_recv.at[half], to_y, half)
            own = pltpu.make_async_copy(held(0, 0), final(0, 0), own_sem)
            own.start()
            own.wait()

        @pl.when((z == half) & (y != 0))
        def _():
            for step in ahead:
                for via in (1, 3):
                    if step % 2 == (via == 1):

                        @pl.when(y == via)
                        def _():
                            slot = step // 2
                            arrived(far_ref.at[slot], far_recv.at[slot])
                            send(
                                far_ref.at[slot], pass_ref.at[step], far_send.at[slot],
                                pass_recv.at[step], 2, half,
                            )

                arrived(pass_ref.at[step], pass_recv.at[step])
                send(
                    pass_ref.at[step], final(y, step), pass_send.at[step],
                    direct_recv.at[half], y, (half + step) % Z_CHIPS,
                )

    for half in range(HALVES):

        @pl.when(chip != half)
        def _():
            arrived(out_ref.at[core, half, rows(chip), :], direct_recv.at[half])

    relay_rings(
        lambda of_core, of_y, of_z: out_ref.at[of_core, :, rows(of_y * Z_CHIPS + of_z), :],
        send_sems,
        recv_sems,
    )
    for half in range(HALVES):

        @pl.when((z == half) & (y == 0))
        def _():
            for slot in range(4 * len(ahead) + 3):
                arrived(pass_ref.at[0], out_send.at[slot])

        @pl.when((z == half) & (y != 0))
        def _():
            for step in ahead:
                arrived(pass_ref.at[step], pass_send.at[step])
                for via in (1, 3):
                    if step % 2 == (via == 1):

                        @pl.when(y == via)
                        def _():
                            arrived(far_ref.at[step // 2], far_send.at[step // 2])


def gram_kernel(
    own_ref, panels_ref, block_ref, out_ref, rhs_ref, part_ref, slots_ref,
    own_sem, row_send, row_recv, send_sems, recv_sems,
):
    core, y, z = ring_places()
    row = lax.axis_index("row")
    height = own_ref.shape[1]
    barrier = pltpu.get_barrier_semaphore()
    for near in (
        col_of(core, y, (z + 1) % Z_CHIPS),
        col_of(core, y, (z + Z_CHIPS - 1) % Z_CHIPS),
        col_of(core, (y + 1) % Y_CHIPS, z),
        col_of(core, (y + Y_CHIPS - 1) % Y_CHIPS, z),
        col_of(1 - core, y, z),
    ):
        pl.semaphore_signal(barrier, inc=1, device_id={"col": near}, device_id_type=MESH)
    for step in range(1, X_CHIPS):
        pl.semaphore_signal(barrier, inc=1, device_id={"row": (row + step) % X_CHIPS}, device_id_type=MESH)

    def panel_dot(left_ref, j):
        return lax.dot_general(
            left_ref[...], panels_ref[j % 2, j // 2], (((0,), (0,)), ((), ())),
            precision=HI, preferred_element_type=jnp.float32,
        )

    def rhs_dot(j):
        rhs_ref[j * B:(j + 1) * B, :] = lax.dot_general(
            panels_ref[j % 2, j // 2], block_ref[...], (((0,), (0,)), ((), ())),
            precision=HI, preferred_element_type=jnp.float32,
        )

    for j in range(P_SIZE):
        part_ref[:, j * B:(j + 1) * B] = panel_dot(own_ref, j)
    pl.semaphore_wait(barrier, 5 + X_CHIPS - 1)
    copies = []
    for step in range(1, X_CHIPS):
        copy = pltpu.make_async_remote_copy(
            src_ref=part_ref,
            dst_ref=slots_ref.at[row],
            send_sem=row_send.at[step],
            recv_sem=row_recv.at[step],
            device_id={"row": (row + step) % X_CHIPS},
            device_id_type=MESH,
        )
        copy.start()
        copies.append(copy)
    own = pltpu.make_async_copy(part_ref, slots_ref.at[row], own_sem)
    own.start()
    own.wait()
    rhs_dot(0)
    rhs_dot(1)
    for step in range(1, X_CHIPS):
        here = slots_ref.at[(row + X_CHIPS - step) % X_CHIPS]
        pltpu.make_async_copy(here, here, row_recv.at[step]).wait()
    total = slots_ref[0]
    for other in range(1, X_CHIPS):
        total = total + slots_ref[other]

    def piece(of_core, of_y, of_z):
        first = pl.multiple_of((of_y * Z_CHIPS + of_z) * height, 8)
        return out_ref.at[of_core, pl.ds(first, height), :]

    piece(core, y, z)[...] = total
    relay_rings(piece, send_sems, recv_sems, (lambda: rhs_dot(2), lambda: rhs_dot(3)))
    for copy in copies:
        copy.wait_send()


def spread_lead(block):
    height, width = block.shape
    chips = Y_CHIPS * Z_CHIPS
    return pl.pallas_call(
        lead_kernel,
        out_shape=jax.ShapeDtypeStruct((2, HALVES, height, width), jnp.float32),
        in_specs=[pl.BlockSpec(memory_space=pltpu.VMEM)],
        out_specs=pl.BlockSpec(memory_space=pltpu.VMEM),
        scratch_shapes=[
            pltpu.VMEM((Z_CHIPS, height // chips, width), jnp.float32),
            pltpu.VMEM((4, height // chips, width), jnp.float32),
            pltpu.SemaphoreType.DMA,
            pltpu.SemaphoreType.DMA((chips,)),
            pltpu.SemaphoreType.DMA((HALVES,)),
            pltpu.SemaphoreType.DMA((Z_CHIPS,)),
            pltpu.SemaphoreType.DMA((4,)),
            pltpu.SemaphoreType.DMA((Z_CHIPS,)),
            pltpu.SemaphoreType.DMA((4,)),
            pltpu.SemaphoreType.DMA((64,)),
            pltpu.SemaphoreType.DMA((64,)),
        ],
        compiler_params=pltpu.CompilerParams(collective_id=0, has_side_effects=True),
        name="spread_lead",
    )(block)


def sum_gram(own, panels, block):
    width = own.shape[1]
    lead = P_SIZE * B
    chips = Y_CHIPS * Z_CHIPS
    return pl.pallas_call(
        gram_kernel,
        out_shape=(
            jax.ShapeDtypeStruct((2, chips * width, lead), jnp.float32),
            jax.ShapeDtypeStruct((lead, B), jnp.float32),
        ),
        in_specs=[pl.BlockSpec(memory_space=pltpu.VMEM)] * 3,
        out_specs=[pl.BlockSpec(memory_space=pltpu.VMEM)] * 2,
        scratch_shapes=[
            pltpu.VMEM((width, lead), jnp.float32),
            pltpu.VMEM((X_CHIPS, width, lead), jnp.float32),
            pltpu.SemaphoreType.DMA,
            pltpu.SemaphoreType.DMA((X_CHIPS,)),
            pltpu.SemaphoreType.DMA((X_CHIPS,)),
            pltpu.SemaphoreType.DMA((64,)),
            pltpu.SemaphoreType.DMA((64,)),
        ],
        compiler_params=pltpu.CompilerParams(collective_id=1, has_side_effects=True),
        name="sum_gram",
    )(own, panels, block)


def on_device(r_slab, arc_rows, arc_blocks):
    n_col = 2 * Y_CHIPS * Z_CHIPS
    col_index = lax.axis_index("col")
    row_index = lax.axis_index("row")
    n_arcs, blocks_here = arc_blocks.shape
    lead = P_SIZE * B
    live = arc_blocks.astype(jnp.float32)
    masked = (arc_rows.reshape(n_arcs, ARC_ROWS, blocks_here, B) * live[:, None, :, None]).reshape(
        arc_rows.shape
    )
    stacked = jnp.concatenate([r_slab, masked], axis=0)
    panels = spread_lead(stacked)
    share = lead // n_col
    row_start = (col_index % 2) * (lead // 2) + (col_index // 2) * share
    block = row_start // B
    own = lax.dynamic_slice(
        panels, (block % 2, block // 2, 0, row_start % B), (1, 1, stacked.shape[0], share)
    )[0, 0]
    gram, rhs = sum_gram(own, panels, stacked)
    mine_out = solve_rows(gram.reshape(lead, lead), rhs)
    row_ids = row_index * B + lax.broadcasted_iota(jnp.int32, (B, B), 0)
    col_ids = col_index * B + lax.broadcasted_iota(jnp.int32, (B, B), 1)
    return jnp.where(col_ids >= row_ids, mine_out, jnp.zeros_like(mine_out))


def solution(mesh):
    return jax.shard_map(
        on_device,
        mesh=mesh,
        in_specs=(P("row", "col"), P("row", "col"), P("row", "col")),
        out_specs=P("row", "col"),
        check_vma=False,
    )
```

```python
import jax
import jax.numpy as jnp
from jax import lax
from jax.experimental import pallas as pl
from jax.experimental.pallas import tpu as pltpu
from jax.sharding import PartitionSpec as P

B = 256
P_SIZE = 4
ARC_ROWS = 128
HI = lax.Precision.HIGHEST
TILE = 128
GROUP = 32
PAIR = 2 * TILE
X_CHIPS, Y_CHIPS, Z_CHIPS = 4, 4, 8
HALVES = 2
MESH = pl.DeviceIdType.MESH


def inner_dot(left, right):
    return lax.dot_general(left, right, (((0,), (0,)), ((), ())), precision=HI)


def plain_dot(left, right):
    return jnp.dot(left, right, precision=HI)


def eliminate_tile(work_ref, inv_ref):
    row_of = lax.broadcasted_iota(jnp.int32, (GROUP, 2 * TILE), 0)
    lane_of = lax.broadcasted_iota(jnp.int32, (GROUP, TILE), 1)
    narrow_row = row_of[:, :TILE]
    for start in range(0, TILE, GROUP):
        panel = work_ref[start:start + GROUP, :]
        spread = [
            jnp.broadcast_to(panel[:, start + i:start + i + 1], (GROUP, TILE)) for i in range(GROUP)
        ]
        left, right = panel[:, :TILE], panel[:, TILE:]
        pivots = jnp.ones((GROUP, TILE), jnp.float32)
        for i in range(GROUP):
            pivot = spread[i][i:i + 1, :]
            pivots = jnp.where(narrow_row == i, jnp.broadcast_to(pivot, pivots.shape), pivots)
            if i + 1 == GROUP:
                break
            scale = jnp.where(narrow_row > i, spread[i], 0.0) * (1.0 / pivot)
            for later in range(i + 1, GROUP):
                spread[later] = spread[later] - scale * spread[later][i:i + 1, :]
            left = left - scale * left[i:i + 1, :]
            right = right - scale * right[i:i + 1, :]
        root = 1.0 / jnp.sqrt(pivots)
        left, right = left * root, right * root
        inv_ref[start:start + GROUP, :] = right
        if start + GROUP < TILE:
            rest = jnp.where(lane_of >= start + GROUP, left, 0.0)
            both = jnp.concatenate([left, right], axis=1)
            work_ref[...] = work_ref[...] - lax.dot_general(
                rest, both, (((0,), (0,)), ((), ())), precision=HI, preferred_element_type=jnp.float32
            )

def invert_blocks(mat_ref, work_ref, inv_ref, first, last):
    tiles = mat_ref.shape[0] // TILE
    eye = jnp.where(
        lax.broadcasted_iota(jnp.int32, (TILE, TILE), 0)
        == lax.broadcasted_iota(jnp.int32, (TILE, TILE), 1), 1.0, 0.0
    ).astype(jnp.float32)

    def step(k, carry):
        at = pl.multiple_of(k * TILE, TILE)
        work_ref[:, :TILE] = mat_ref[pl.ds(at, TILE), pl.ds(at, TILE)]
        work_ref[:, TILE:] = eye
        eliminate_tile(work_ref, inv_ref)
        mat_ref[pl.ds(at, TILE), pl.ds(at, TILE)] = eye
        mat_ref[pl.ds(at, TILE), :] = jnp.dot(
            inv_ref[...], mat_ref[pl.ds(at, TILE), :], precision=HI, preferred_element_type=jnp.float32
        )

        def update(i, inner):
            below = pl.multiple_of(i * PAIR, PAIR)
            rows_here = below + lax.broadcasted_iota(jnp.int32, (PAIR, TILE), 0)
            lanes_here = below + lax.broadcasted_iota(jnp.int32, (TILE, PAIR), 1)
            old = mat_ref[pl.ds(below, PAIR), pl.ds(at, TILE)]
            mat_ref[pl.ds(below, PAIR), pl.ds(at, TILE)] = jnp.where(rows_here >= at + TILE, 0.0, old)
            factor = mat_ref[pl.ds(at, TILE), pl.ds(below, PAIR)]
            mat_ref[pl.ds(below, PAIR), :] = mat_ref[pl.ds(below, PAIR), :] - lax.dot_general(
                jnp.where(lanes_here >= at + TILE, factor, 0.0),
                mat_ref[pl.ds(at, TILE), :],
                (((0,), (0,)), ((), ())),
                precision=HI,
                preferred_element_type=jnp.float32,
            )
            return inner

        lax.fori_loop((k + 1) // 2, tiles // 2, update, 0)
        return carry

    lax.fori_loop(first, last, step, 0)


def solve_kernel(
    gram_ref, rhs_ref, out_ref, mat_ref, work_ref, inv_ref, slots_ref, sum_ref, own_sem,
    part_send, part_recv, sum_send, sum_recv,
):
    row = lax.axis_index("row")
    size = gram_ref.shape[0]
    height = size // X_CHIPS
    barrier = pltpu.get_barrier_semaphore()
    for step in range(1, X_CHIPS):
        pl.semaphore_signal(barrier, inc=1, device_id={"row": (row + step) % X_CHIPS}, device_id_type=MESH)
    mat_ref[...] = gram_ref[...]
    pl.semaphore_wait(barrier, X_CHIPS - 1)

    def rows(of_row):
        return pl.ds(pl.multiple_of(of_row * height, 8), height)

    copies = []
    for step in range(1, X_CHIPS):
        peer = (row + step) % X_CHIPS
        copy = pltpu.make_async_remote_copy(
            src_ref=rhs_ref.at[rows(peer), :],
            dst_ref=slots_ref.at[row],
            send_sem=part_send.at[step],
            recv_sem=part_recv.at[step],
            device_id={"row": peer},
            device_id_type=MESH,
        )
        copy.start()
        copies.append(copy)
    own = pltpu.make_async_copy(rhs_ref.at[rows(row), :], slots_ref.at[row], own_sem)
    own.start()
    own.wait()
    invert_blocks(mat_ref, work_ref, inv_ref, 0, size // TILE // 2)
    for step in range(1, X_CHIPS):
        here = slots_ref.at[(row + X_CHIPS - step) % X_CHIPS]
        pltpu.make_async_copy(here, here, part_recv.at[step]).wait()
    total = slots_ref[0]
    for other in range(1, X_CHIPS):
        total = total + slots_ref[other]
    sum_ref[rows(row), :] = total
    for step in range(1, X_CHIPS):
        copy = pltpu.make_async_remote_copy(
            src_ref=sum_ref.at[rows(row), :],
            dst_ref=sum_ref.at[rows(row), :],
            send_sem=sum_send.at[step],
            recv_sem=sum_recv.at[step],
            device_id={"row": (row + step) % X_CHIPS},
            device_id_type=MESH,
        )
        copy.start()
        copies.append(copy)
    invert_blocks(mat_ref, work_ref, inv_ref, size // TILE // 2, size // TILE)
    for step in range(1, X_CHIPS):
        here = sum_ref.at[rows((row + X_CHIPS - step) % X_CHIPS), :]
        pltpu.make_async_copy(here, here, sum_recv.at[step]).wait()
    tile_row = (row * height + lax.broadcasted_iota(jnp.int32, (height, size), 0)) // TILE
    tile_col = lax.broadcasted_iota(jnp.int32, (height, size), 1) // TILE
    inverse = jnp.where(tile_col <= tile_row, mat_ref[rows(row), :], 0.0)
    out_ref[...] = jnp.dot(inverse, sum_ref[...], precision=HI, preferred_element_type=jnp.float32)
    for copy in copies:
        copy.wait_send()


def solve_rows(gram, rhs):
    size = gram.shape[0]
    height = size // X_CHIPS
    return pl.pallas_call(
        solve_kernel,
        out_shape=jax.ShapeDtypeStruct((height, rhs.shape[1]), jnp.float32),
        in_specs=[pl.BlockSpec(memory_space=pltpu.VMEM)] * 2,
        out_specs=pl.BlockSpec(memory_space=pltpu.VMEM),
        scratch_shapes=[
            pltpu.VMEM((size, size), jnp.float32),
            pltpu.VMEM((TILE, 2 * TILE), jnp.float32),
            pltpu.VMEM((TILE, TILE), jnp.float32),
            pltpu.VMEM((X_CHIPS, height, rhs.shape[1]), jnp.float32),
            pltpu.VMEM(rhs.shape, jnp.float32),
            pltpu.SemaphoreType.DMA,
            pltpu.SemaphoreType.DMA((X_CHIPS,)),
            pltpu.SemaphoreType.DMA((X_CHIPS,)),
            pltpu.SemaphoreType.DMA((X_CHIPS,)),
            pltpu.SemaphoreType.DMA((X_CHIPS,)),
        ],
        compiler_params=pltpu.CompilerParams(collective_id=2, has_side_effects=True),
        name="solve_rows",
    )(gram, rhs)


def ring_places():
    me = lax.axis_index("col")
    return me % 2, me // 2 // Z_CHIPS, (me // 2) % Z_CHIPS


def col_of(core, y, z):
    return (y * Z_CHIPS + z) * 2 + core


def relay_rings(piece, send_sems, recv_sems, fill=()):
    core, y, z = ring_places()
    sent = []

    def pass_on(slot, src_y, src_z, to):
        copy = pltpu.make_async_remote_copy(
            src_ref=piece(core, src_y, src_z),
            dst_ref=piece(core, src_y, src_z),
            send_sem=send_sems.at[slot],
            recv_sem=recv_sems.at[slot],
            device_id={"col": to},
            device_id_type=MESH,
        )
        copy.start()
        sent.append(copy)

    def arrived(slot, src_core, src_y, src_z):
        here = piece(src_core, src_y, src_z)
        pltpu.make_async_copy(here, here, recv_sems.at[slot]).wait()

    z_up, z_down = (z + 1) % Z_CHIPS, (z + Z_CHIPS - 1) % Z_CHIPS
    y_up, y_down = (y + 1) % Y_CHIPS, (y + Y_CHIPS - 1) % Y_CHIPS
    y_far = (y + 2) % Y_CHIPS
    twin = col_of(1 - core, y, z)
    slots_z, slots_up, slots_down, slots_far, slots_twin = 0, 8, 16, 24, 32
    order = [0, 1, 7, 2, 6, 3, 5, 4]

    def source(back):
        return (z + Z_CHIPS - back) % Z_CHIPS

    def spread_y(back):
        pass_on(slots_up + back, y, source(back), col_of(core, y_up, z))
        pass_on(slots_down + back, y, source(back), col_of(core, y_down, z))
        pass_on(slots_twin + back, y, source(back), twin)

    def spread_far(back):
        arrived(slots_up + back, core, y_down, source(back))
        if back % 2 == 0:
            pass_on(slots_far + back, y_down, source(back), col_of(core, y_up, z))
        pass_on(slots_twin + 8 + back, y_down, source(back), twin)
        arrived(slots_down + back, core, y_up, source(back))
        if back % 2 == 1:
            pass_on(slots_far + back, y_up, source(back), col_of(core, y_down, z))
        pass_on(slots_twin + 16 + back, y_up, source(back), twin)

    def spread_twin(back):
        arrived(slots_far + back, core, y_far, source(back))
        pass_on(slots_twin + 24 + back, y_far, source(back), twin)

    pass_on(slots_z + 1, y, z, col_of(core, y, z_up))
    pass_on(slots_z + 7, y, z, col_of(core, y, z_down))
    spread_y(0)
    for work in fill[:1]:
        work()
    for at, back in enumerate(order):
        if back:
            arrived(slots_z + back, core, y, source(back))
            if back < 4:
                pass_on(slots_z + back + 1, y, source(back), col_of(core, y, z_up))
            if back > 5:
                pass_on(slots_z + back - 1, y, source(back), col_of(core, y, z_down))
            spread_y(back)
        if at >= 2:
            spread_far(order[at - 2])
        if at >= 4:
            spread_twin(order[at - 4])
    for back in order[6:]:
        spread_far(back)
    for back in order[4:]:
        spread_twin(back)
    for work in fill[1:]:
        work()
    for back in order:
        for kind, src_y in enumerate((y, y_down, y_up, y_far)):
            arrived(slots_twin + 8 * kind + back, 1 - core, src_y, source(back))
    for copy in sent:
        copy.wait_send()


def lead_kernel(
    block_ref, out_ref, pass_ref, far_ref, own_sem, out_send, direct_recv, pass_recv, far_recv,
    pass_send, far_send, send_sems, recv_sems,
):
    core, y, z = ring_places()
    chip = y * Z_CHIPS + z
    chips = Y_CHIPS * Z_CHIPS
    height = block_ref.shape[0] // chips
    barrier = pltpu.get_barrier_semaphore()

    def greet(step, carry):
        other = (chip + step) % chips
        pl.semaphore_signal(barrier, inc=1, device_id={"col": other * 2 + core}, device_id_type=MESH)
        return carry

    lax.fori_loop(1, chips, greet, 0)
    pl.semaphore_signal(barrier, inc=1, device_id={"col": chip * 2 + 1 - core}, device_id_type=MESH)
    pl.semaphore_wait(barrier, chips)

    def rows(of_chip):
        return pl.ds(pl.multiple_of(of_chip * height, 8), height)

    def send(source, target, send_sem, recv_sem, to_y, to_z):
        copy = pltpu.make_async_remote_copy(
            src_ref=source, dst_ref=target, send_sem=send_sem, recv_sem=recv_sem,
            device_id={"col": col_of(core, to_y, to_z)}, device_id_type=MESH,
        )
        copy.start()
        return copy

    def arrived(here, sem):
        pltpu.make_async_copy(here, here, sem).wait()

    ahead = (4, 3, 5, 2, 6, 1, 7)
    for half in range(HALVES):

        def place(of_y, step):
            return of_y * Z_CHIPS + (half + step) % Z_CHIPS

        def final(of_y, step):
            return out_ref.at[core, half, rows(place(of_y, step)), :]

        @pl.when((z == half) & (y == 0))
        def _():
            slots = iter(range(chips))

            def push(source, target, recv_sem, to_y, to_z):
                send(source, target, out_send.at[next(slots)], recv_sem, to_y, to_z)

            def held(of_y, step):
                return block_ref.at[rows(place(of_y, step)), :]

            for step in ahead:
                via, slot = (1, step // 2) if step % 2 else (3, step // 2)
                push(held(2, step), far_ref.at[slot], far_recv.at[slot], via, half)
                for to_y in (1, 3):
                    push(held(to_y, step), pass_ref.at[step], pass_recv.at[step], to_y, half)
                to_z = (half + step) % Z_CHIPS
                push(held(0, step), final(0, step), direct_recv.at[half], 0, to_z)
            for to_y in (2, 1, 3):
                push(held(to_y, 0), final(to_y, 0), direct_recv.at[half], to_y, half)
            own = pltpu.make_async_copy(held(0, 0), final(0, 0), own_sem)
            own.start()
            own.wait()

        @pl.when((z == half) & (y != 0))
        def _():
            for step in ahead:
                for via in (1, 3):
                    if step % 2 == (via == 1):

                        @pl.when(y == via)
                        def _():
                            slot = step // 2
                            arrived(far_ref.at[slot], far_recv.at[slot])
                            send(
                                far_ref.at[slot], pass_ref.at[step], far_send.at[slot],
                                pass_recv.at[step], 2, half,
                            )

                arrived(pass_ref.at[step], pass_recv.at[step])
                send(
                    pass_ref.at[step], final(y, step), pass_send.at[step],
                    direct_recv.at[half], y, (half + step) % Z_CHIPS,
                )

    for half in range(HALVES):

        @pl.when(chip != half)
        def _():
            arrived(out_ref.at[core, half, rows(chip), :], direct_recv.at[half])

    relay_rings(
        lambda of_core, of_y, of_z: out_ref.at[of_core, :, rows(of_y * Z_CHIPS + of_z), :],
        send_sems,
        recv_sems,
    )
    for half in range(HALVES):

        @pl.when((z == half) & (y == 0))
        def _():
            for slot in range(4 * len(ahead) + 3):
                arrived(pass_ref.at[0], out_send.at[slot])

        @pl.when((z == half) & (y != 0))
        def _():
            for step in ahead:
                arrived(pass_ref.at[step], pass_send.at[step])
                for via in (1, 3):
                    if step % 2 == (via == 1):

                        @pl.when(y == via)
                        def _():
                            arrived(far_ref.at[step // 2], far_send.at[step // 2])


def gram_kernel(
    own_ref, panels_ref, block_ref, out_ref, rhs_ref, part_ref, slots_ref,
    own_sem, row_send, row_recv, send_sems, recv_sems,
):
    core, y, z = ring_places()
    row = lax.axis_index("row")
    height = own_ref.shape[1]
    barrier = pltpu.get_barrier_semaphore()
    for near in (
        col_of(core, y, (z + 1) % Z_CHIPS),
        col_of(core, y, (z + Z_CHIPS - 1) % Z_CHIPS),
        col_of(core, (y + 1) % Y_CHIPS, z),
        col_of(core, (y + Y_CHIPS - 1) % Y_CHIPS, z),
        col_of(1 - core, y, z),
    ):
        pl.semaphore_signal(barrier, inc=1, device_id={"col": near}, device_id_type=MESH)
    for step in range(1, X_CHIPS):
        pl.semaphore_signal(barrier, inc=1, device_id={"row": (row + step) % X_CHIPS}, device_id_type=MESH)

    def panel_dot(left_ref, j):
        return lax.dot_general(
            left_ref[...], panels_ref[j % 2, j // 2], (((0,), (0,)), ((), ())),
            precision=HI, preferred_element_type=jnp.float32,
        )

    def rhs_dot(j):
        rhs_ref[j * B:(j + 1) * B, :] = lax.dot_general(
            panels_ref[j % 2, j // 2], block_ref[...], (((0,), (0,)), ((), ())),
            precision=HI, preferred_element_type=jnp.float32,
        )

    for j in range(P_SIZE):
        part_ref[:, j * B:(j + 1) * B] = panel_dot(own_ref, j)
    pl.semaphore_wait(barrier, 5 + X_CHIPS - 1)
    copies = []
    for step in range(1, X_CHIPS):
        copy = pltpu.make_async_remote_copy(
            src_ref=part_ref,
            dst_ref=slots_ref.at[row],
            send_sem=row_send.at[step],
            recv_sem=row_recv.at[step],
            device_id={"row": (row + step) % X_CHIPS},
            device_id_type=MESH,
        )
        copy.start()
        copies.append(copy)
    own = pltpu.make_async_copy(part_ref, slots_ref.at[row], own_sem)
    own.start()
    own.wait()
    rhs_dot(0)
    rhs_dot(1)
    for step in range(1, X_CHIPS):
        here = slots_ref.at[(row + X_CHIPS - step) % X_CHIPS]
        pltpu.make_async_copy(here, here, row_recv.at[step]).wait()
    total = slots_ref[0]
    for other in range(1, X_CHIPS):
        total = total + slots_ref[other]

    def piece(of_core, of_y, of_z):
        first = pl.multiple_of((of_y * Z_CHIPS + of_z) * height, 8)
        return out_ref.at[of_core, pl.ds(first, height), :]

    piece(core, y, z)[...] = total
    relay_rings(piece, send_sems, recv_sems, (lambda: rhs_dot(2), lambda: rhs_dot(3)))
    for copy in copies:
        copy.wait_send()


def spread_lead(block):
    height, width = block.shape
    chips = Y_CHIPS * Z_CHIPS
    return pl.pallas_call(
        lead_kernel,
        out_shape=jax.ShapeDtypeStruct((2, HALVES, height, width), jnp.float32),
        in_specs=[pl.BlockSpec(memory_space=pltpu.VMEM)],
        out_specs=pl.BlockSpec(memory_space=pltpu.VMEM),
        scratch_shapes=[
            pltpu.VMEM((Z_CHIPS, height // chips, width), jnp.float32),
            pltpu.VMEM((4, height // chips, width), jnp.float32),
            pltpu.SemaphoreType.DMA,
            pltpu.SemaphoreType.DMA((chips,)),
            pltpu.SemaphoreType.DMA((HALVES,)),
            pltpu.SemaphoreType.DMA((Z_CHIPS,)),
            pltpu.SemaphoreType.DMA((4,)),
            pltpu.SemaphoreType.DMA((Z_CHIPS,)),
            pltpu.SemaphoreType.DMA((4,)),
            pltpu.SemaphoreType.DMA((64,)),
            pltpu.SemaphoreType.DMA((64,)),
        ],
        compiler_params=pltpu.CompilerParams(collective_id=0, has_side_effects=True),
        name="spread_lead",
    )(block)


def sum_gram(own, panels, block):
    width = own.shape[1]
    lead = P_SIZE * B
    chips = Y_CHIPS * Z_CHIPS
    return pl.pallas_call(
        gram_kernel,
        out_shape=(
            jax.ShapeDtypeStruct((2, chips * width, lead), jnp.float32),
            jax.ShapeDtypeStruct((lead, B), jnp.float32),
        ),
        in_specs=[pl.BlockSpec(memory_space=pltpu.VMEM)] * 3,
        out_specs=[pl.BlockSpec(memory_space=pltpu.VMEM)] * 2,
        scratch_shapes=[
            pltpu.VMEM((width, lead), jnp.float32),
            pltpu.VMEM((X_CHIPS, width, lead), jnp.float32),
            pltpu.SemaphoreType.DMA,
            pltpu.SemaphoreType.DMA((X_CHIPS,)),
            pltpu.SemaphoreType.DMA((X_CHIPS,)),
            pltpu.SemaphoreType.DMA((64,)),
            pltpu.SemaphoreType.DMA((64,)),
        ],
        compiler_params=pltpu.CompilerParams(collective_id=1, has_side_effects=True),
        name="sum_gram",
    )(own, panels, block)


def on_device(r_slab, arc_rows, arc_blocks):
    n_col = 2 * Y_CHIPS * Z_CHIPS
    col_index = lax.axis_index("col")
    row_index = lax.axis_index("row")
    n_arcs, blocks_here = arc_blocks.shape
    lead = P_SIZE * B
    live = arc_blocks.astype(jnp.float32)
    masked = (arc_rows.reshape(n_arcs, ARC_ROWS, blocks_here, B) * live[:, None, :, None]).reshape(
        arc_rows.shape
    )
    stacked = jnp.concatenate([r_slab, masked], axis=0)
    panels = spread_lead(stacked)
    share = lead // n_col
    row_start = (col_index % 2) * (lead // 2) + (col_index // 2) * share
    block = row_start // B
    own = lax.dynamic_slice(
        panels, (block % 2, block // 2, 0, row_start % B), (1, 1, stacked.shape[0], share)
    )[0, 0]
    gram, rhs = sum_gram(own, panels, stacked)
    mine_out = solve_rows(gram.reshape(lead, lead), rhs)
    row_ids = row_index * B + lax.broadcasted_iota(jnp.int32, (B, B), 0)
    col_ids = col_index * B + lax.broadcasted_iota(jnp.int32, (B, B), 1)
    return jnp.where(col_ids >= row_ids, mine_out, jnp.zeros_like(mine_out))


def solution(mesh):
    return jax.shard_map(
        on_device,
        mesh=mesh,
        in_specs=(P("row", "col"), P("row", "col"), P("row", "col")),
        out_specs=P("row", "col"),
        check_vma=False,
    )
```
